256 devices in a mesh: pole: 8 (over x, y_lo), sub: 32 (over y_hi, z, core).
Axes of the slice: x: 4, y: 4 (y_hi: 2, y_lo: 2; y = y_hi * 2 + y_lo), z: 8, core: 2. Of those that a mesh axis runs over, the one named last changes fastest.
Arguments:
- start_block: float32 [131072, 128], P('sub'), may hold values from -400 to 400
- inverses: float32 [8, 256, 512, 512], P('pole', 'sub'), may hold values from -1 to 3
- iface_rows: int32 [256, 2, 128], P('sub'), may hold values from 0 to 511, as said below
- neighbors: int32 [256, 2], P('sub'), may hold values from 0 to 255, as said below
- couplings: float32 [256, 2, 128], P('sub'), may hold values from 0.25 to 1
- pole_weights: float32 [8], P('pole'), may hold values from 0.25 to 1
Outputs:
- ortho_basis: float32 [131072, 128], P(('sub', 'pole'))
The draws below stay inside these ranges and needn't reach their ends.
Inputs may be any that keep to these rules, and one draw needn't show every extreme that they name: `iface_rows`: in each subdomain the 256 listed rows are distinct. Subdomain j lies on index j // 8 of sub. neighbors[j, 0] lies on the previous index and neighbors[j, 1] on the next one, cyclically; over the subdomains of one index, the values in column 0 are the previous index's 8 subdomains, each once, and those in column 1 the next index's, each once.
All inputs are finite; a program needn't handle non-finite values.
Results may differ from the reference program's by a relative error of at most 0.0002.
Values sent between devices are 32-bit elements; how exact they have to be, the bound alone decides.
A program may use at most 64 MiB of HBM per device.

```python
import math
import jax
import jax.numpy as jnp
from jax import lax

BLOCK = 512
VECS = 128
IFACE = 128
SUB_DEV = 8
SUBS = 256
NROWS = 131072
POLES = 8


def draw_start_block(key, part):
    noise_key, row_key, col_key = jax.random.split(key, 3)
    position = jnp.arange(NROWS, dtype=jnp.float32) / NROWS
    entries = jax.random.truncated_normal(noise_key, -4.0, 4.0, (NROWS, VECS), jnp.float32)
    row_scale = jnp.exp(jax.random.uniform(row_key, (NROWS, 1), jnp.float32, 0.0, math.log(10.0)))
    row_scale = row_scale * (1.0 + 2.0 * position)[:, None]
    col_scale = jnp.exp(jax.random.uniform(col_key, (1, VECS), jnp.float32, 0.0, math.log(10.0)))
    return 0.1 * entries * row_scale * col_scale


def draw_inverses(key, part):
    noise_key, diag_key = jax.random.split(key, 2)
    full_shape = (POLES, SUBS, BLOCK, BLOCK)
    spread = 0.4 * jax.random.truncated_normal(noise_key, -4.0, 4.0, full_shape, jnp.float32) / math.sqrt(BLOCK)
    diagonal = jax.random.uniform(diag_key, (POLES, SUBS, 1, BLOCK), jnp.float32, 0.5, 1.5)
    return spread + jnp.eye(BLOCK, dtype=jnp.float32) * diagonal


def draw_iface_rows(key, part):
    keys = jax.random.split(jax.random.fold_in(key, 21), SUBS)
    orders = jax.vmap(lambda single: jax.random.permutation(single, BLOCK))(keys)
    return orders[:, :2 * IFACE].reshape(SUBS, 2, IFACE).astype(jnp.int32)


def draw_neighbors(key, part):
    groups = SUBS // SUB_DEV
    low_keys = jax.random.split(jax.random.fold_in(key, 31), groups)
    high_keys = jax.random.split(jax.random.fold_in(key, 32), groups)
    low_order = jax.vmap(lambda single: jax.random.permutation(single, SUB_DEV))(low_keys)
    high_order = jax.vmap(lambda single: jax.random.permutation(single, SUB_DEV))(high_keys)
    device_ids = jnp.arange(groups, dtype=jnp.int32)[:, None]
    before = (device_ids - 1) % groups * SUB_DEV + low_order
    following = (device_ids + 1) % groups * SUB_DEV + high_order
    return jnp.stack([before.reshape(-1), following.reshape(-1)], axis=1).astype(jnp.int32)


def steps_of(stream_key, shape, cuts, low, top_value):
    gain = 1.0
    for dim, blocks in cuts:
        heights = jax.random.uniform(jax.random.fold_in(jax.random.fold_in(stream_key, 6), dim), (blocks,), jnp.float32, low / len(cuts), top_value / len(cuts))
        gain = gain * jnp.repeat(jnp.exp(heights), shape[dim] // blocks).reshape((-1,) + (1,) * (len(shape) - 1 - dim))
    return gain


def setup_inputs(seed: int = 0) -> dict:
    arg_keys = jax.random.split(jax.random.key(seed), 7)
    start_block = draw_start_block(jax.random.fold_in(arg_keys[6], 71), 0)
    inverses = draw_inverses(jax.random.fold_in(arg_keys[6], 71), 0)
    iface_rows = draw_iface_rows(jax.random.fold_in(arg_keys[6], 71), 0)
    neighbors = draw_neighbors(jax.random.fold_in(arg_keys[6], 71), 0)
    couplings = jnp.clip(jnp.exp(math.log(1.0) - 1.3862944 * jax.random.uniform(arg_keys[4], (SUBS, 2, IFACE), jnp.float32) ** steps_of(arg_keys[4], (SUBS, 2, IFACE), ((0, 32),), -0.2, 0.2)), 0.25, 1.0)
    pole_weights = jnp.clip(0.25 + 0.75 * jax.random.uniform(arg_keys[5], (POLES,), jnp.float32) ** steps_of(arg_keys[5], (POLES,), ((0, 8),), -0.2, 0.2), 0.25, 1.0)
    return {"start_block": start_block, "inverses": inverses, "iface_rows": iface_rows, "neighbors": neighbors, "couplings": couplings, "pole_weights": pole_weights}


precise = lax.Precision.HIGHEST

def apply_blocks(blocks, fields):
    return jnp.einsum('sij,sjv->siv', blocks.astype(jnp.float32), fields.astype(jnp.float32), precision=precise, preferred_element_type=jnp.float32)

def add_coupled(fields, iface_rows, neighbor_vals, couplings):

    def one_sub(field_one, rows_one, terms_one):
        field_one = field_one.at[rows_one[0]].add(terms_one[0])
        return field_one.at[rows_one[1]].add(terms_one[1])
    return jax.vmap(one_sub)(fields, iface_rows, couplings[..., None] * neighbor_vals)

def reference(start_block, inverses, iface_rows, neighbors, couplings, pole_weights):
    fields = start_block.reshape(SUBS, BLOCK, VECS)
    offsets = (jnp.arange(SUBS, dtype=jnp.int32) * BLOCK)[:, None, None]
    flat_index = (iface_rows + offsets).reshape(-1).astype(jnp.int32)

    def one_pole(summed_poles, pole_in):
        blocks, weight = pole_in
        first_pass = apply_blocks(blocks, fields)
        side_rows = jnp.take(first_pass.reshape(NROWS, VECS), flat_index, axis=0).reshape(SUBS, 2, IFACE, VECS)
        low_terms = side_rows[neighbors[:, 0], 1]
        high_terms = side_rows[neighbors[:, 1], 0]
        corrected = add_coupled(fields, iface_rows, jnp.stack([low_terms, high_terms], 1), couplings)
        return (summed_poles + weight * apply_blocks(blocks, corrected), None)
    summed_poles, leftover = lax.scan(one_pole, jnp.zeros((SUBS, BLOCK, VECS), jnp.float32), (inverses, pole_weights))
    filtered = summed_poles.reshape(NROWS, VECS)
    gram_matrix = jnp.dot(filtered.T.astype(jnp.float32), filtered.astype(jnp.float32), precision=precise, preferred_element_type=jnp.float32)
    lower_factor = jnp.linalg.cholesky(gram_matrix)
    solved = lax.linalg.triangular_solve(lower_factor, filtered, left_side=False, lower=True, transpose_a=True)
    return math.sqrt(NROWS) * solved
```

```python
import functools
import math

import jax
import jax.numpy as jnp
from jax import lax
from jax.experimental import pallas as pl
from jax.experimental.pallas import tpu as pltpu
from jax.sharding import PartitionSpec as P

precise = lax.Precision.HIGHEST
MESH = pl.DeviceIdType.MESH
F32 = jnp.float32
BF16 = jnp.bfloat16

SUB = 8
BLK = 512
VEC = 128
IFC = 128
HALF = BLK // 2
NX = 4
NSUB = 32


def pair(value):
    high = value.astype(BF16)
    low = (value - high.astype(F32)).astype(BF16)
    return jnp.concatenate([high, low], axis=1)


def fold(wide):
    return wide[:, :VEC] + wide[:, VEC:]


def mm(a, b):
    return jnp.dot(a, b, preferred_element_type=F32)


def down_lanes(row):
    return jnp.broadcast_to(row, (IFC, IFC)).T


def filter_kernel(
    nb_ref, w_ref, rows_ref, coup_ref, start_ref, inv_ref, out_ref,
    a32, ahl, b32, outgoing, arrived, term, far_l, far_r, near_l, near_r, from_y,
    a_sem, b_sem, ex_send, ex_recv, far_send, far_recv, near_send, near_recv, y_send, y_recv,
):
    pole = lax.axis_index("pole")
    sub = lax.axis_index("sub")
    x = pole // 2
    yl = pole % 2
    other = 1 - yl
    nxt = (sub + 1) % NSUB
    prv = (sub + NSUB - 1) % NSUB
    right = ((x + 1) % NX) * 2 + yl
    left = ((x + NX - 1) % NX) * 2 + yl
    across = x * 2 + other

    def fetch(s):
        return pltpu.make_async_copy(inv_ref.at[s], a32.at[s], a_sem.at[s])

    fetch_b = pltpu.make_async_copy(start_ref, b32, b_sem)
    fetch_b.start()
    for s in range(SUB):
        fetch(s).start()

    barrier = pltpu.get_barrier_semaphore()
    for dev in ((pole, nxt), (pole, prv), (right, sub), (left, sub), (across, sub)):
        pl.semaphore_signal(barrier, inc=1, device_id=dev, device_id_type=MESH)
    pl.semaphore_wait(barrier, 5)
    fetch_b.wait()

    def exchange(side, s):
        return pltpu.make_async_remote_copy(
            src_ref=outgoing.at[side, s],
            dst_ref=arrived.at[1 - side, s],
            send_sem=ex_send.at[side, s],
            recv_sem=ex_recv.at[1 - side, s],
            device_id=(pole, prv if side == 0 else nxt),
            device_id_type=MESH,
        )

    lane_ids = lax.broadcasted_iota(jnp.int32, (IFC, BLK), 1).astype(F32)
    row_ids = lax.broadcasted_iota(jnp.int32, (BLK, 2 * IFC), 0)

    def first(s, carry):
        fetch(s).wait()
        a = a32[s]
        high = a.astype(BF16)
        ahl[s, :, :BLK] = high
        ahl[s, :, BLK:] = (a - high.astype(F32)).astype(BF16)
        b = pair(b32[s])
        first_pass = fold(mm(ahl[s], jnp.concatenate([b, b], axis=0)))
        parts = pair(first_pass)
        rows = rows_ref[s].astype(F32)
        for side in range(2):
            ids = down_lanes(rows[side : side + 1])
            pick = (lane_ids == jnp.concatenate([ids] * (BLK // IFC), axis=1)).astype(F32).astype(BF16)
            outgoing[side, s] = fold(mm(pick, parts))
            exchange(side, s).start()
        return carry

    lax.fori_loop(0, SUB, first, 0)

    def arrive(s, carry):
        exchange(0, s).wait()
        exchange(1, s).wait()
        return carry

    lax.fori_loop(0, SUB, arrive, 0)

    weight = w_ref[0]

    def second(s):
        rows = rows_ref[s]
        coup = coup_ref[s]
        low = arrived[0, lax.rem(nb_ref[s, 0], SUB)] * down_lanes(coup[0:1])
        high = arrived[1, lax.rem(nb_ref[s, 1], SUB)] * down_lanes(coup[1:2])
        terms = pair(jnp.concatenate([low, high], axis=0))
        row = jnp.concatenate([rows[0:1], rows[1:2]], axis=1)
        place = (row_ids == row).astype(F32).astype(BF16)
        corrected = b32[s] + fold(mm(place, terms))
        c = pair(corrected)
        term[s] = weight * fold(mm(ahl[s], jnp.concatenate([c, c], axis=0)))

    lo = pl.ds(0, HALF)
    hi = pl.ds(HALF, HALF)

    def owner(shift, kind):
        return ((x + shift) % NX) * 2 + (other if kind == 0 else yl)

    def send(src, dst, s_sem, r_sem, dev):
        return pltpu.make_async_remote_copy(
            src_ref=src, dst_ref=dst, send_sem=s_sem, recv_sem=r_sem,
            device_id=(dev, sub), device_id_type=MESH,
        )

    def far(kind):
        s = owner(2, kind)
        return (
            send(term.at[s, lo], far_l.at[kind], far_send.at[0, kind], far_recv.at[0, kind], right),
            send(term.at[s, hi], far_r.at[kind], far_send.at[1, kind], far_recv.at[1, kind], left),
        )

    def near(kind, step):
        to_r = hi if step == 0 else lo
        to_l = lo if step == 0 else hi
        return (
            send(term.at[owner(1, kind), to_r], near_l.at[kind, to_r], near_send.at[0, kind, step],
                 near_recv.at[0, kind, step], right),
            send(term.at[owner(3, kind), to_l], near_r.at[kind, to_l], near_send.at[1, kind, step],
                 near_recv.at[1, kind, step], left),
        )

    def sequence(i, carry):
        shift = jnp.where(i < 2, 2, jnp.where(i < 6, 1 + 2 * (i % 2), 0))
        kind = jnp.where(i < 2, i, jnp.where(i < 6, (i - 2) // 2, i - 6))
        s = ((x + shift) % NX) * 2 + jnp.where(kind == 0, other, yl)
        second(s)
        for n in range(2):
            @pl.when(i == n)
            def _():
                for copy in far(n):
                    copy.start()

        @pl.when(i == 2)
        def _():
            near(0, 0)[0].start()

        @pl.when(i == 3)
        def _():
            near(0, 0)[1].start()
        return carry

    lax.fori_loop(0, SUB, sequence, 0)

    def relay(kind):
        far_a, far_b = far(kind)
        s = owner(1, kind)
        far_a.wait_recv()
        term[s, lo] = term[s, lo] + far_l[kind]
        near(kind, 1)[0].start()
        s = owner(3, kind)
        far_b.wait_recv()
        term[s, hi] = term[s, hi] + far_r[kind]
        near(kind, 1)[1].start()

    relay(0)
    for copy in near(1, 0):
        copy.start()
    relay(1)

    def gathered(kind):
        for step in range(2):
            for copy in near(kind, step):
                copy.wait_recv()
        s = owner(0, kind)
        return term[s] + near_l[kind] + near_r[kind]

    term[owner(0, 0)] = gathered(0)
    hand = send(term.at[owner(0, 0)], from_y, y_send, y_recv, across)
    hand.start()
    mine = gathered(1)
    hand.wait_recv()
    out_ref[...] = mine + from_y[...]
    hand.wait_send()
    for kind in range(2):
        for copy in far(kind) + near(kind, 0) + near(kind, 1):
            copy.wait_send()


def filter_call(neighbors, pole_weights, iface_rows, couplings, start, inverses):
    dma = pltpu.SemaphoreType.DMA
    vmem = pl.BlockSpec(memory_space=pltpu.VMEM)
    smem = pl.BlockSpec(memory_space=pltpu.SMEM)
    hbm = pl.BlockSpec(memory_space=pl.ANY)
    return pl.pallas_call(
        filter_kernel,
        name="filter_pass",
        out_shape=jax.ShapeDtypeStruct((BLK, VEC), F32),
        in_specs=[smem, smem, vmem, vmem, hbm, hbm],
        out_specs=vmem,
        scratch_shapes=[
            pltpu.VMEM((SUB, BLK, BLK), F32),
            pltpu.VMEM((SUB, BLK, 2 * BLK), BF16),
            pltpu.VMEM((SUB, BLK, VEC), F32),
            pltpu.VMEM((2, SUB, IFC, VEC), F32),
            pltpu.VMEM((2, SUB, IFC, VEC), F32),
            pltpu.VMEM((SUB, BLK, VEC), F32),
            pltpu.VMEM((2, HALF, VEC), F32),
            pltpu.VMEM((2, HALF, VEC), F32),
            pltpu.VMEM((2, BLK, VEC), F32),
            pltpu.VMEM((2, BLK, VEC), F32),
            pltpu.VMEM((BLK, VEC), F32),
            dma((SUB,)),
            dma,
            dma((2, SUB)),
            dma((2, SUB)),
            dma((2, 2)),
            dma((2, 2)),
            dma((2, 2, 2)),
            dma((2, 2, 2)),
            dma,
            dma,
        ],
        compiler_params=pltpu.CompilerParams(
            collective_id=0, has_side_effects=True, vmem_limit_bytes=56 * 1024 * 1024
        ),
    )(neighbors, pole_weights, iface_rows, couplings, start, inverses)


PIECE = VEC // 8


def gram_kernel(
    f_ref, out_ref,
    local, part, s2, s3, s4, acc2, acc3, full,
    send2, recv2, send3, recv3, send4, recv4, send5, recv5,
):
    pole = lax.axis_index("pole")
    sub = lax.axis_index("sub")
    x = pole // 2
    yl = pole % 2
    yh = sub // 16
    z = (sub // 2) % 8
    core = sub % 2
    y = yh * 2 + yl
    here = x * 2 + core

    def at_xc(d):
        t = (here + d) % 8
        return t, ((t // 2) * 2 + yl, (yh * 8 + z) * 2 + t % 2)

    def at_y(d):
        t = (y + d) % 4
        return (x * 2 + t % 2, ((t // 2) * 8 + z) * 2 + core)

    def at_z(d):
        t = (z + d) % 8
        return (pole, (yh * 8 + t) * 2 + core)

    barrier = pltpu.get_barrier_semaphore()
    for d in range(1, 8):
        pl.semaphore_signal(barrier, inc=1, device_id=at_xc(d)[1], device_id_type=MESH)
        pl.semaphore_signal(barrier, inc=1, device_id=at_z(d), device_id_type=MESH)
    for d in range(1, 4):
        pl.semaphore_signal(barrier, inc=1, device_id=at_y(d), device_id_type=MESH)

    f = f_ref[...]
    local[...] = lax.dot_general(
        f, f, (((0,), (0,)), ((), ())), precision=precise, preferred_element_type=F32
    )
    pl.semaphore_wait(barrier, 17)

    def send(src, dst, s_sem, r_sem, dev):
        return pltpu.make_async_remote_copy(
            src_ref=src, dst_ref=dst, send_sem=s_sem, recv_sem=r_sem,
            device_id=dev, device_id_type=MESH,
        )

    def rows(n):
        return pl.ds(pl.multiple_of(n * PIECE, PIECE), PIECE)

    copies = []
    for d in range(1, 8):
        t, dev = at_xc(d)
        copies.append(send(local.at[rows(t)], s2.at[d - 1], send2.at[d - 1], recv2.at[d - 1], dev))
    for copy in copies:
        copy.start()
    total = local[rows(here)]
    for d in range(7):
        copies[d].wait_recv()
        total = total + s2[d]
    acc2[...] = total

    copies3 = [
        send(acc2, s3.at[d - 1], send3.at[d - 1], recv3.at[d - 1], at_y(d)) for d in range(1, 4)
    ]
    for copy in copies3:
        copy.start()
    for d in range(3):
        copies3[d].wait_recv()
        total = total + s3[d]
    acc3[...] = total

    copies4 = [
        send(acc3, s4.at[d - 1], send4.at[d - 1], recv4.at[d - 1], at_z(d)) for d in range(1, 8)
    ]
    for copy in copies4:
        copy.start()
    for d in range(7):
        copies4[d].wait_recv()
        total = total + s4[d]
    part[...] = total

    copies5 = [
        send(part, full.at[rows(here)], send5.at[d - 1], recv5.at[d - 1], at_xc(d)[1])
        for d in range(1, 8)
    ]
    for copy in copies5:
        copy.start()
    out_ref[rows(here)] = total
    for d in range(1, 8):
        t = (here + 8 - d) % 8
        copies5[d - 1].wait_recv()
        out_ref[rows(t)] = full[rows(t)]
    for copy in copies + copies3 + copies4 + copies5:
        copy.wait_send()


def gram_call(filtered):
    dma = pltpu.SemaphoreType.DMA
    vmem = pl.BlockSpec(memory_space=pltpu.VMEM)
    return pl.pallas_call(
        gram_kernel,
        name="gram_sum",
        out_shape=jax.ShapeDtypeStruct((VEC, VEC), F32),
        in_specs=[vmem],
        out_specs=vmem,
        scratch_shapes=[
            pltpu.VMEM((VEC, VEC), F32),
            pltpu.VMEM((PIECE, VEC), F32),
            pltpu.VMEM((7, PIECE, VEC), F32),
            pltpu.VMEM((3, PIECE, VEC), F32),
            pltpu.VMEM((7, PIECE, VEC), F32),
            pltpu.VMEM((PIECE, VEC), F32),
            pltpu.VMEM((PIECE, VEC), F32),
            pltpu.VMEM((VEC, VEC), F32),
            dma((7,)), dma((7,)), dma((3,)), dma((3,)),
            dma((7,)), dma((7,)), dma((7,)), dma((7,)),
        ],
        compiler_params=pltpu.CompilerParams(collective_id=1, has_side_effects=True),
    )(filtered)


def per_device(start_block, inverses, iface_rows, neighbors, couplings, pole_weights):
    filtered = filter_call(
        neighbors, pole_weights, iface_rows, couplings,
        start_block.reshape(SUB, BLK, VEC), inverses[0],
    )
    gram_matrix = gram_call(filtered)
    lower_factor = jnp.linalg.cholesky(gram_matrix)
    solved = lax.linalg.triangular_solve(
        lower_factor, filtered, left_side=False, lower=True, transpose_a=True
    )
    return math.sqrt(NSUB * SUB * BLK) * solved


def solution(mesh):
    placed = (
        P("sub", None),
        P("pole", "sub", None, None),
        P("sub", None, None),
        P("sub", None),
        P("sub", None, None),
        P("pole"),
    )
    return jax.shard_map(
        per_device, mesh=mesh, in_specs=placed, out_specs=P(("sub", "pole"), None), check_vma=False
    )
```

```python
import functools
import math

import jax
import jax.numpy as jnp
from jax import lax
from jax.experimental import pallas as pl
from jax.experimental.pallas import tpu as pltpu
from jax.sharding import PartitionSpec as P

precise = lax.Precision.HIGHEST
MESH = pl.DeviceIdType.MESH
F32 = jnp.float32
BF16 = jnp.bfloat16

SUB = 8
BLK = 512
VEC = 128
IFC = 128
HALF = BLK // 2
NX = 4
NSUB = 32


def pair(value):
    high = value.astype(BF16)
    low = (value - high.astype(F32)).astype(BF16)
    return jnp.concatenate([high, low], axis=1)


def fold(wide):
    return wide[:, :VEC] + wide[:, VEC:]


def mm(a, b):
    return jnp.dot(a, b, preferred_element_type=F32)


def down_lanes(row):
    return jnp.broadcast_to(row, (IFC, IFC)).T


def filter_kernel(
    nb_hbm, w_ref, rows_ref, coup_ref, start_ref, inv_ref, out_ref, gram_ref,
    nb_ref, a32, ahl, b32, outgoing, arrived, term, far_l, far_r, near_l, near_r, from_y,
    local, slot2, slot3, slot4, acc2, acc3, part,
    a_sem, b_sem, nb_sem, ex_send, ex_recv, far_send, far_recv, near_send, near_recv,
    y_send, y_recv, send2, recv2, send3, recv3, send4, recv4, send5, recv5,
):
    pole = lax.axis_index("pole")
    sub = lax.axis_index("sub")
    x = pole // 2
    yl = pole % 2
    other = 1 - yl
    yh = sub // 16
    z = (sub // 2) % 8
    core = sub % 2
    y = yh * 2 + yl
    here = x * 2 + core
    nxt = (sub + 1) % NSUB
    prv = (sub + NSUB - 1) % NSUB
    right = ((x + 1) % NX) * 2 + yl
    left = ((x + NX - 1) % NX) * 2 + yl
    across = x * 2 + other

    def at_xc(d):
        t = (here + d) % 8
        return t, ((t // 2) * 2 + yl, (yh * 8 + z) * 2 + t % 2)

    def at_y(d):
        t = (y + d) % 4
        return (x * 2 + t % 2, ((t // 2) * 8 + z) * 2 + core)

    def at_z(d):
        t = (z + d) % 8
        return (pole, (yh * 8 + t) * 2 + core)

    def fetch(s):
        return (
            pltpu.make_async_copy(inv_ref.at[s], a32.at[s], a_sem.at[s]),
            pltpu.make_async_copy(start_ref.at[s], b32.at[s], b_sem.at[s]),
        )

    fetch_nb = pltpu.make_async_copy(nb_hbm, nb_ref, nb_sem)
    for s in range(SUB):
        for copy in fetch(s):
            copy.start()
    fetch_nb.start()

    barrier = pltpu.get_barrier_semaphore()
    peers = [(pole, nxt), (pole, prv)]
    peers += [at_xc(d)[1] for d in range(1, 8)]
    peers += [at_y(d) for d in range(1, 4)]
    peers += [at_z(d) for d in range(1, 8)]
    for dev in peers:
        pl.semaphore_signal(barrier, inc=1, device_id=dev, device_id_type=MESH)

    def send(src, dst, s_sem, r_sem, dev):
        return pltpu.make_async_remote_copy(
            src_ref=src, dst_ref=dst, send_sem=s_sem, recv_sem=r_sem,
            device_id=dev, device_id_type=MESH,
        )

    def exchange(side, s):
        return send(
            outgoing.at[side, s], arrived.at[1 - side, s],
            ex_send.at[side, s], ex_recv.at[1 - side, s],
            (pole, prv if side == 0 else nxt),
        )

    lane_ids = lax.broadcasted_iota(jnp.int32, (IFC, BLK), 1).astype(F32)
    row_ids = lax.broadcasted_iota(jnp.int32, (BLK, 2 * IFC), 0)

    def apply(s, vectors):
        parts = pair(vectors)
        return fold(mm(ahl[s, :, :BLK], parts)) + mm(ahl[s, :, BLK:], parts[:, :VEC])

    def first(s, carry):
        for copy in fetch(s):
            copy.wait()
        a = a32[s]
        high = a.astype(BF16)
        ahl[s, :, :BLK] = high
        ahl[s, :, BLK:] = (a - high.astype(F32)).astype(BF16)
        parts = pair(apply(s, b32[s]))
        rows = rows_ref[s].astype(F32)
        for side in range(2):
            ids = down_lanes(rows[side : side + 1])
            pick = (lane_ids == jnp.concatenate([ids] * (BLK // IFC), axis=1)).astype(F32).astype(BF16)
            outgoing[side, s] = fold(mm(pick, parts))

        @pl.when(s == 0)
        def _():
            pl.semaphore_wait(barrier, len(peers))

        for side in range(2):
            exchange(side, s).start()
        return carry

    lax.fori_loop(0, SUB, first, 0)
    fetch_nb.wait()

    def arrive(s, carry):
        exchange(0, s).wait()
        exchange(1, s).wait()
        return carry

    lax.fori_loop(0, SUB, arrive, 0)

    weight = w_ref[0]

    def second(s):
        rows = rows_ref[s]
        coup = coup_ref[s]
        low = arrived[0, lax.rem(nb_ref[0, s], SUB)] * down_lanes(coup[0:1])
        high = arrived[1, lax.rem(nb_ref[1, s], SUB)] * down_lanes(coup[1:2])
        terms = pair(jnp.concatenate([low, high], axis=0))
        row = jnp.concatenate([rows[0:1], rows[1:2]], axis=1)
        place = (row_ids == row).astype(F32).astype(BF16)
        term[s] = weight * apply(s, b32[s] + fold(mm(place, terms)))

    lo = pl.ds(0, HALF)
    hi = pl.ds(HALF, HALF)

    def owner(shift, kind):
        return ((x + shift) % NX) * 2 + (other if kind == 0 else yl)

    def far(kind):
        s = owner(2, kind)
        return (
            send(term.at[s, lo], far_l.at[kind], far_send.at[0, kind], far_recv.at[0, kind], (right, sub)),
            send(term.at[s, hi], far_r.at[kind], far_send.at[1, kind], far_recv.at[1, kind], (left, sub)),
        )

    def near(kind, step):
        to_r = hi if step == 0 else lo
        to_l = lo if step == 0 else hi
        return (
            send(term.at[owner(1, kind), to_r], near_l.at[kind, to_r], near_send.at[0, kind, step],
                 near_recv.at[0, kind, step], (right, sub)),
            send(term.at[owner(3, kind), to_l], near_r.at[kind, to_l], near_send.at[1, kind, step],
                 near_recv.at[1, kind, step], (left, sub)),
        )

    def sequence(i, carry):
        shift = jnp.where(i < 2, 2, jnp.where(i < 6, 1 + 2 * (i % 2), 0))
        kind = jnp.where(i < 2, i, jnp.where(i < 6, (i - 2) // 2, i - 6))
        second(((x + shift) % NX) * 2 + jnp.where(kind == 0, other, yl))
        for n in range(2):
            @pl.when(i == n)
            def _():
                for copy in far(n):
                    copy.start()

        @pl.when(i == 2)
        def _():
            near(0, 0)[0].start()

        @pl.when(i == 3)
        def _():
            near(0, 0)[1].start()
        return carry

    lax.fori_loop(0, SUB, sequence, 0)

    def relay(kind):
        far_a, far_b = far(kind)
        s = owner(1, kind)
        far_a.wait_recv()
        term[s, lo] = term[s, lo] + far_l[kind]
        near(kind, 1)[0].start()
        s = owner(3, kind)
        far_b.wait_recv()
        term[s, hi] = term[s, hi] + far_r[kind]
        near(kind, 1)[1].start()

    relay(0)
    for copy in near(1, 0):
        copy.start()
    relay(1)

    def gathered(kind):
        for step in range(2):
            for copy in near(kind, step):
                copy.wait_recv()
        return term[owner(0, kind)] + near_l[kind] + near_r[kind]

    term[owner(0, 0)] = gathered(0)
    hand = send(term.at[owner(0, 0)], from_y, y_send, y_recv, (across, sub))
    hand.start()
    mine = gathered(1)
    hand.wait_recv()
    mine = mine + from_y[...]
    out_ref[...] = mine

    parts = pair(mine)
    four = lax.dot_general(parts, parts, (((0,), (0,)), ((), ())), preferred_element_type=F32)
    local[...] = fold(four[:VEC]) + fold(four[VEC:])

    def rows_of(n):
        return pl.ds(pl.multiple_of(n * PIECE, PIECE), PIECE)

    copies2 = []
    for d in range(1, 8):
        t, dev = at_xc(d)
        copies2.append(send(local.at[rows_of(t)], slot2.at[d - 1], send2.at[d - 1], recv2.at[d - 1], dev))
    for copy in copies2:
        copy.start()
    total = local[rows_of(here)]
    for d in range(7):
        copies2[d].wait_recv()
        total = total + slot2[d]
    acc2[...] = total

    copies3 = [
        send(acc2, slot3.at[d - 1], send3.at[d - 1], recv3.at[d - 1], at_y(d)) for d in range(1, 4)
    ]
    for copy in copies3:
        copy.start()
    for d in range(3):
        copies3[d].wait_recv()
        total = total + slot3[d]
    acc3[...] = total

    copies4 = [
        send(acc3, slot4.at[d - 1], send4.at[d - 1], recv4.at[d - 1], at_z(d)) for d in range(1, 8)
    ]
    for copy in copies4:
        copy.start()
    for d in range(7):
        copies4[d].wait_recv()
        total = total + slot4[d]
    part[...] = total
    gram_ref[rows_of(here)] = total

    copies5 = [
        send(part, gram_ref.at[rows_of(here)], send5.at[d - 1], recv5.at[d - 1], at_xc(d)[1])
        for d in range(1, 8)
    ]
    for copy in copies5:
        copy.start()
    hand.wait_send()
    for kind in range(2):
        for copy in far(kind) + near(kind, 0) + near(kind, 1):
            copy.wait_send()
    for copy in copies2 + copies3 + copies4:
        copy.wait_send()
    for copy in copies5:
        copy.wait()


PIECE = VEC // 8


def filter_call(neighbors, pole_weights, iface_rows, couplings, start, inverses):
    dma = pltpu.SemaphoreType.DMA
    vmem = pl.BlockSpec(memory_space=pltpu.VMEM)
    smem = pl.BlockSpec(memory_space=pltpu.SMEM)
    hbm = pl.BlockSpec(memory_space=pl.ANY)
    return pl.pallas_call(
        filter_kernel,
        name="filter_pass",
        out_shape=(
            jax.ShapeDtypeStruct((BLK, VEC), F32),
            jax.ShapeDtypeStruct((VEC, VEC), F32),
        ),
        in_specs=[hbm, smem, vmem, vmem, hbm, hbm],
        out_specs=(vmem, vmem),
        scratch_shapes=[
            pltpu.SMEM((2, SUB), jnp.int32),
            pltpu.VMEM((SUB, BLK, BLK), F32),
            pltpu.VMEM((SUB, BLK, 2 * BLK), BF16),
            pltpu.VMEM((SUB, BLK, VEC), F32),
            pltpu.VMEM((2, SUB, IFC, VEC), F32),
            pltpu.VMEM((2, SUB, IFC, VEC), F32),
            pltpu.VMEM((SUB, BLK, VEC), F32),
            pltpu.VMEM((2, HALF, VEC), F32),
            pltpu.VMEM((2, HALF, VEC), F32),
            pltpu.VMEM((2, BLK, VEC), F32),
            pltpu.VMEM((2, BLK, VEC), F32),
            pltpu.VMEM((BLK, VEC), F32),
            pltpu.VMEM((VEC, VEC), F32),
            pltpu.VMEM((7, PIECE, VEC), F32),
            pltpu.VMEM((3, PIECE, VEC), F32),
            pltpu.VMEM((7, PIECE, VEC), F32),
            pltpu.VMEM((PIECE, VEC), F32),
            pltpu.VMEM((PIECE, VEC), F32),
            pltpu.VMEM((PIECE, VEC), F32),
            dma((SUB,)), dma((SUB,)), dma,
            dma((2, SUB)), dma((2, SUB)),
            dma((2, 2)), dma((2, 2)),
            dma((2, 2, 2)), dma((2, 2, 2)),
            dma, dma,
            dma((7,)), dma((7,)), dma((3,)), dma((3,)),
            dma((7,)), dma((7,)), dma((7,)), dma((7,)),
        ],
        compiler_params=pltpu.CompilerParams(
            collective_id=0, has_side_effects=True, vmem_limit_bytes=56 * 1024 * 1024
        ),
    )(neighbors, pole_weights, iface_rows, couplings, start, inverses)


TILE = 8


def spread(row):
    return jnp.broadcast_to(row, (TILE, VEC))


def ortho_kernel(scale, g_ref, f_ref, out_ref, w_ref):
    count = VEC // TILE
    tiles = [g_ref[TILE * t : TILE * t + TILE, :] for t in range(count)]
    sub = lax.broadcasted_iota(jnp.int32, (TILE, VEC), 0)
    lane = lax.broadcasted_iota(jnp.int32, (TILE, VEC), 1)
    for p in range(count):
        c0 = TILE * p
        cols = {
            (m, t): jnp.broadcast_to(tiles[t][:, c0 + m : c0 + m + 1], (TILE, VEC))
            for t in range(p, count)
            for m in range(TILE)
        }
        panel = (lane >= c0) & (lane < c0 + TILE)
        pivots = jnp.ones((TILE, VEC), F32)
        top = jnp.where(panel, (lane - c0 == sub).astype(F32), tiles[p])
        factors = {}
        for k in range(TILE):
            pivot = spread(cols[k, p][k : k + 1])
            pivots = jnp.where(sub == k, pivot, pivots)
            inverse = 1.0 / pivot
            upper = {m: spread(cols[m, p][k : k + 1]) for m in range(k + 1, TILE)}
            f = jnp.where(sub > k, cols[k, p] * inverse, 0.0)
            for m in range(k + 1, TILE):
                cols[m, p] = cols[m, p] - f * upper[m]
            top = top - f * spread(top[k : k + 1])
            for t in range(p + 1, count):
                f = cols[k, t] * inverse
                factors[k, t] = f
                for m in range(k + 1, TILE):
                    cols[m, t] = cols[m, t] - f * upper[m]
        rows = [spread(top[k : k + 1]) for k in range(TILE)]
        for t in range(p + 1, count):
            value = jnp.where(panel, 0.0, tiles[t])
            for k in range(TILE):
                value = value - factors[k, t] * rows[k]
            tiles[t] = value
        w_ref[c0 : c0 + TILE, :] = jnp.where(lane <= sub + c0, top * (scale * lax.rsqrt(pivots)), 0.0)
    out_ref[...] = lax.dot_general(
        f_ref[...], w_ref[...], (((1,), (1,)), ((), ())), precision=precise, preferred_element_type=F32
    )


def ortho_call(gram_matrix, filtered, scale):
    vmem = pl.BlockSpec(memory_space=pltpu.VMEM)
    return pl.pallas_call(
        functools.partial(ortho_kernel, scale),
        name="ortho",
        out_shape=jax.ShapeDtypeStruct((BLK, VEC), F32),
        in_specs=[vmem, vmem],
        out_specs=vmem,
        scratch_shapes=[pltpu.VMEM((VEC, VEC), F32)],
    )(gram_matrix, filtered)


def per_device(start_block, inverses, iface_rows, neighbors, couplings, pole_weights):
    filtered, gram_matrix = filter_call(
        neighbors.T, pole_weights, iface_rows, couplings,
        start_block.reshape(SUB, BLK, VEC), inverses[0],
    )
    return ortho_call(gram_matrix, filtered, math.sqrt(NSUB * SUB * BLK))


def solution(mesh):
    placed = (
        P("sub", None),
        P("pole", "sub", None, None),
        P("sub", None, None),
        P("sub", None),
        P("sub", None, None),
        P("pole"),
    )
    return jax.shard_map(
        per_device, mesh=mesh, in_specs=placed, out_specs=P(("sub", "pole"), None), check_vma=False
    )
```

```python
import functools
import math

import jax
import jax.numpy as jnp
from jax import lax
from jax.experimental import pallas as pl
from jax.experimental.pallas import tpu as pltpu
from jax.sharding import PartitionSpec as P

precise = lax.Precision.HIGHEST
MESH = pl.DeviceIdType.MESH
F32 = jnp.float32
BF16 = jnp.bfloat16

SUB = 8
BLK = 512
VEC = 128
IFC = 128
XROWS = 288
YROWS = BLK - XROWS
NX = 4
NSUB = 32


def pair(value):
    high = value.astype(BF16)
    low = (value - high.astype(F32)).astype(BF16)
    return jnp.concatenate([high, low], axis=1)


def fold(wide):
    return wide[:, :VEC] + wide[:, VEC:]


def mm(a, b):
    return jnp.dot(a, b, preferred_element_type=F32)


def down_lanes(row):
    return jnp.broadcast_to(row, (IFC, IFC)).T


def filter_kernel(
    nb_hbm, w_ref, rows_ref, coup_ref, start_ref, inv_ref, out_ref, gram_ref,
    nb_ref, a32, ahl, b32, outgoing, arrived, term, far_l, far_r, far_l2, far_r2, near_l, near_r, crossed, from_y,
    local, slot2, slot3, slot4, acc2, acc3, part,
    a_sem, b_sem, nb_sem, ex_send, ex_recv, far_send, far_recv, near_send, near_recv,
    cross_send, cross_recv, y_send, y_recv, send2, recv2, send3, recv3, send4, recv4, send5, recv5,
):
    pole = lax.axis_index("pole")
    sub = lax.axis_index("sub")
    x = pole // 2
    yl = pole % 2
    other = 1 - yl
    yh = sub // 16
    z = (sub // 2) % 8
    core = sub % 2
    y = yh * 2 + yl
    here = x * 2 + core
    nxt = (sub + 1) % NSUB
    prv = (sub + NSUB - 1) % NSUB
    right = ((x + 1) % NX) * 2 + yl
    left = ((x + NX - 1) % NX) * 2 + yl
    across = x * 2 + other

    def at_xc(d):
        t = (here + d) % 8
        return t, ((t // 2) * 2 + yl, (yh * 8 + z) * 2 + t % 2)

    def at_y(d):
        t = (y + d) % 4
        return (x * 2 + t % 2, ((t // 2) * 8 + z) * 2 + core)

    def at_z(d):
        t = (z + d) % 8
        return (pole, (yh * 8 + t) * 2 + core)

    def fetch(s):
        return (
            pltpu.make_async_copy(inv_ref.at[s], a32.at[s], a_sem.at[s]),
            pltpu.make_async_copy(start_ref.at[s], b32.at[s], b_sem.at[s]),
        )

    fetch_nb = pltpu.make_async_copy(nb_hbm, nb_ref, nb_sem)
    for s in range(SUB):
        for copy in fetch(s):
            copy.start()
    fetch_nb.start()

    barrier = pltpu.get_barrier_semaphore()
    peers = [(pole, nxt), (pole, prv)]
    peers += [at_xc(d)[1] for d in range(1, 8)]
    peers += [at_y(d) for d in range(1, 4)]
    peers += [at_z(d) for d in range(1, 8)]
    for dev in peers:
        pl.semaphore_signal(barrier, inc=1, device_id=dev, device_id_type=MESH)

    def send(src, dst, s_sem, r_sem, dev):
        return pltpu.make_async_remote_copy(
            src_ref=src, dst_ref=dst, send_sem=s_sem, recv_sem=r_sem,
            device_id=dev, device_id_type=MESH,
        )

    def exchange(side, s):
        return send(
            outgoing.at[side, s], arrived.at[1 - side, s],
            ex_send.at[side, s], ex_recv.at[1 - side, s],
            (pole, prv if side == 0 else nxt),
        )

    lane_ids = lax.broadcasted_iota(jnp.int32, (IFC, BLK), 1).astype(F32)
    row_ids = lax.broadcasted_iota(jnp.int32, (BLK, 2 * IFC), 0)

    def apply(s, vectors):
        parts = pair(vectors)
        return fold(mm(ahl[s, :, :BLK], parts)) + mm(ahl[s, :, BLK:], parts[:, :VEC])

    def first(s, carry):
        for copy in fetch(s):
            copy.wait()
        a = a32[s]
        high = a.astype(BF16)
        ahl[s, :, :BLK] = high
        ahl[s, :, BLK:] = (a - high.astype(F32)).astype(BF16)
        parts = pair(apply(s, b32[s]))
        rows = rows_ref[s].astype(F32)
        for side in range(2):
            ids = down_lanes(rows[side : side + 1])
            pick = (lane_ids == jnp.concatenate([ids] * (BLK // IFC), axis=1)).astype(F32).astype(BF16)
            outgoing[side, s] = fold(mm(pick, parts))

        @pl.when(s == 0)
        def _():
            pl.semaphore_wait(barrier, len(peers))

        for side in range(2):
            exchange(side, s).start()
        return carry

    lax.fori_loop(0, SUB, first, 0)
    fetch_nb.wait()

    def arrive(s, carry):
        exchange(0, s).wait()
        exchange(1, s).wait()
        return carry

    lax.fori_loop(0, SUB, arrive, 0)

    weight = w_ref[0]

    def second(s):
        rows = rows_ref[s]
        coup = coup_ref[s]
        low = arrived[0, lax.rem(nb_ref[0, s], SUB)] * down_lanes(coup[0:1])
        high = arrived[1, lax.rem(nb_ref[1, s], SUB)] * down_lanes(coup[1:2])
        terms = pair(jnp.concatenate([low, high], axis=0))
        row = jnp.concatenate([rows[0:1], rows[1:2]], axis=1)
        place = (row_ids == row).astype(F32).astype(BF16)
        term[s] = weight * apply(s, b32[s] + fold(mm(place, terms)))

    def owner(shift, kind):
        return ((x + shift) % NX) * 2 + (other if kind == 0 else yl)

    lo, hi = pl.ds(0, XROWS // 2), pl.ds(XROWS // 2, XROWS // 2)
    ylo, yhi = pl.ds(XROWS, YROWS // 2), pl.ds(XROWS + YROWS // 2, YROWS // 2)
    xrows, yrows = pl.ds(0, XROWS), pl.ds(XROWS, YROWS)

    def far(kind):
        s = owner(2, min(kind, 1))
        to_r, to_l = (lo, hi) if kind < 2 else (ylo, yhi)
        dst_r = far_l.at[kind] if kind < 2 else far_l2
        dst_l = far_r.at[kind] if kind < 2 else far_r2
        return (
            send(term.at[s, to_r], dst_r, far_send.at[0, kind], far_recv.at[0, kind], (right, sub)),
            send(term.at[s, to_l], dst_l, far_send.at[1, kind], far_recv.at[1, kind], (left, sub)),
        )

    def near(kind, step):
        low, high = (lo, hi) if kind < 2 else (ylo, yhi)
        to_r, to_l = (high, low) if step == 0 else (low, high)
        s, slot = min(kind, 1), min(kind, 1)
        return (
            send(term.at[owner(1, s), to_r], near_l.at[slot, to_r], near_send.at[0, kind, step],
                 near_recv.at[0, kind, step], (right, sub)),
            send(term.at[owner(3, s), to_l], near_r.at[slot, to_l], near_send.at[1, kind, step],
                 near_recv.at[1, kind, step], (left, sub)),
        )

    def cross(shift):
        return send(
            term.at[owner(shift, 0), yrows], crossed.at[shift],
            cross_send.at[shift], cross_recv.at[shift], (across, sub),
        )

    def relay(kind):
        far_a, far_b = far(kind)
        low, high = (lo, hi) if kind < 2 else (ylo, yhi)
        s = owner(1, min(kind, 1))
        far_a.wait_recv()
        term[s, low] = term[s, low] + (far_l[kind] if kind < 2 else far_l2[...])
        near(kind, 1)[0].start()
        s = owner(3, min(kind, 1))
        far_b.wait_recv()
        term[s, high] = term[s, high] + (far_r[kind] if kind < 2 else far_r2[...])
        near(kind, 1)[1].start()

    def join(shift):
        cross(shift).wait_recv()
        s = owner(shift, 1)
        term[s, yrows] = term[s, yrows] + crossed[shift]

    def sequence(i, carry):
        shift = jnp.where(i < 2, 2, jnp.where(i < 5, (2 * i - 3) % 4, (2 * i - 9) % 4))
        shift = jnp.where((i == 4) | (i == 7), 0, shift)
        kind = jnp.where((i == 1) | (i > 4), 1, 0)

        @pl.when(i == 7)
        def _():
            relay(0)

        second(((x + shift) % NX) * 2 + jnp.where(kind == 0, other, yl))

        @pl.when(i == 0)
        def _():
            far(0)[0].start()
            far(0)[1].start()
            cross(2).start()

        @pl.when(i == 1)
        def _():
            far(1)[0].start()
            far(1)[1].start()

        @pl.when(i == 2)
        def _():
            near(0, 0)[0].start()
            cross(1).start()

        @pl.when(i == 3)
        def _():
            near(0, 0)[1].start()
            cross(3).start()

        @pl.when(i == 4)
        def _():
            cross(0).start()
        return carry

    lax.fori_loop(0, SUB, sequence, 0)

    join(2)
    for copy in far(2) + near(1, 0):
        copy.start()
    relay(1)
    join(1)
    near(2, 0)[0].start()
    join(3)
    near(2, 0)[1].start()

    own = owner(0, 0)
    for copy in near(0, 0) + near(0, 1):
        copy.wait_recv()
    term[own, xrows] = term[own, xrows] + near_l[0, xrows] + near_r[0, xrows]
    hand = send(term.at[own, xrows], from_y, y_send, y_recv, (across, sub))
    hand.start()
    relay(2)
    join(0)
    for copy in near(1, 0) + near(1, 1) + near(2, 0) + near(2, 1):
        copy.wait_recv()
    own = owner(0, 1)
    hand.wait_recv()
    term[own, xrows] = term[own, xrows] + from_y[...]
    mine = term[own] + near_l[1] + near_r[1]
    out_ref[...] = mine

    parts = pair(mine)
    four = lax.dot_general(parts, parts, (((0,), (0,)), ((), ())), preferred_element_type=F32)
    local[...] = fold(four[:VEC]) + fold(four[VEC:])

    def rows_of(n):
        return pl.ds(pl.multiple_of(n * PIECE, PIECE), PIECE)

    copies2 = []
    for d in range(1, 8):
        t, dev = at_xc(d)
        copies2.append(send(local.at[rows_of(t)], slot2.at[d - 1], send2.at[d - 1], recv2.at[d - 1], dev))
    for copy in copies2:
        copy.start()
    total = local[rows_of(here)]
    for d in range(7):
        copies2[d].wait_recv()
        total = total + slot2[d]
    acc2[...] = total

    copies3 = [
        send(acc2, slot3.at[d - 1], send3.at[d - 1], recv3.at[d - 1], at_y(d)) for d in range(1, 4)
    ]
    for copy in copies3:
        copy.start()
    for d in range(3):
        copies3[d].wait_recv()
        total = total + slot3[d]
    acc3[...] = total

    copies4 = [
        send(acc3, slot4.at[d - 1], send4.at[d - 1], recv4.at[d - 1], at_z(d)) for d in range(1, 8)
    ]
    for copy in copies4:
        copy.start()
    for d in range(7):
        copies4[d].wait_recv()
        total = total + slot4[d]
    part[...] = total
    gram_ref[rows_of(here)] = total

    copies5 = [
        send(part, gram_ref.at[rows_of(here)], send5.at[d - 1], recv5.at[d - 1], at_xc(d)[1])
        for d in range(1, 8)
    ]
    for copy in copies5:
        copy.start()
    hand.wait_send()
    for kind in range(3):
        for copy in far(kind) + near(kind, 0) + near(kind, 1):
            copy.wait_send()
    for shift in range(NX):
        cross(shift).wait_send()
    for copy in copies2 + copies3 + copies4:
        copy.wait_send()
    for copy in copies5:
        copy.wait()


PIECE = VEC // 8


def filter_call(neighbors, pole_weights, iface_rows, couplings, start, inverses):
    dma = pltpu.SemaphoreType.DMA
    vmem = pl.BlockSpec(memory_space=pltpu.VMEM)
    smem = pl.BlockSpec(memory_space=pltpu.SMEM)
    hbm = pl.BlockSpec(memory_space=pl.ANY)
    return pl.pallas_call(
        filter_kernel,
        name="filter_pass",
        out_shape=(
            jax.ShapeDtypeStruct((BLK, VEC), F32),
            jax.ShapeDtypeStruct((VEC, VEC), F32),
        ),
        in_specs=[hbm, smem, vmem, vmem, hbm, hbm],
        out_specs=(vmem, vmem),
        scratch_shapes=[
            pltpu.SMEM((2, SUB), jnp.int32),
            pltpu.VMEM((SUB, BLK, BLK), F32),
            pltpu.VMEM((SUB, BLK, 2 * BLK), BF16),
            pltpu.VMEM((SUB, BLK, VEC), F32),
            pltpu.VMEM((2, SUB, IFC, VEC), F32),
            pltpu.VMEM((2, SUB, IFC, VEC), F32),
            pltpu.VMEM((SUB, BLK, VEC), F32),
            pltpu.VMEM((2, XROWS // 2, VEC), F32),
            pltpu.VMEM((2, XROWS // 2, VEC), F32),
            pltpu.VMEM((YROWS // 2, VEC), F32),
            pltpu.VMEM((YROWS // 2, VEC), F32),
            pltpu.VMEM((2, BLK, VEC), F32),
            pltpu.VMEM((2, BLK, VEC), F32),
            pltpu.VMEM((NX, YROWS, VEC), F32),
            pltpu.VMEM((XROWS, VEC), F32),
            pltpu.VMEM((VEC, VEC), F32),
            pltpu.VMEM((7, PIECE, VEC), F32),
            pltpu.VMEM((3, PIECE, VEC), F32),
            pltpu.VMEM((7, PIECE, VEC), F32),
            pltpu.VMEM((PIECE, VEC), F32),
            pltpu.VMEM((PIECE, VEC), F32),
            pltpu.VMEM((PIECE, VEC), F32),
            dma((SUB,)), dma((SUB,)), dma,
            dma((2, SUB)), dma((2, SUB)),
            dma((2, 3)), dma((2, 3)),
            dma((2, 3, 2)), dma((2, 3, 2)),
            dma((NX,)), dma((NX,)), dma, dma,
            dma((7,)), dma((7,)), dma((3,)), dma((3,)),
            dma((7,)), dma((7,)), dma((7,)), dma((7,)),
        ],
        compiler_params=pltpu.CompilerParams(
            collective_id=0, has_side_effects=True, vmem_limit_bytes=56 * 1024 * 1024
        ),
    )(neighbors, pole_weights, iface_rows, couplings, start, inverses)


TILE = 8


def spread(row):
    return jnp.broadcast_to(row, (TILE, VEC))


def ortho_kernel(scale, g_ref, f_ref, out_ref, w_ref):
    count = VEC // TILE
    tiles = [g_ref[TILE * t : TILE * t + TILE, :] for t in range(count)]
    sub = lax.broadcasted_iota(jnp.int32, (TILE, VEC), 0)
    lane = lax.broadcasted_iota(jnp.int32, (TILE, VEC), 1)
    for p in range(count):
        c0 = TILE * p
        cols = {
            (m, t): jnp.broadcast_to(tiles[t][:, c0 + m : c0 + m + 1], (TILE, VEC))
            for t in range(p, count)
            for m in range(TILE)
        }
        panel = (lane >= c0) & (lane < c0 + TILE)
        pivots = jnp.ones((TILE, VEC), F32)
        top = jnp.where(panel, (lane - c0 == sub).astype(F32), tiles[p])
        factors = {}
        for k in range(TILE):
            pivot = spread(cols[k, p][k : k + 1])
            pivots = jnp.where(sub == k, pivot, pivots)
            inverse = 1.0 / pivot
            upper = {m: spread(cols[m, p][k : k + 1]) for m in range(k + 1, TILE)}
            f = jnp.where(sub > k, cols[k, p] * inverse, 0.0)
            for m in range(k + 1, TILE):
                cols[m, p] = cols[m, p] - f * upper[m]
            top = top - f * spread(top[k : k + 1])
            for t in range(p + 1, count):
                f = cols[k, t] * inverse
                factors[k, t] = f
                for m in range(k + 1, TILE):
                    cols[m, t] = cols[m, t] - f * upper[m]
        rows = [spread(top[k : k + 1]) for k in range(TILE)]
        for t in range(p + 1, count):
            value = jnp.where(panel, 0.0, tiles[t])
            for k in range(TILE):
                value = value - factors[k, t] * rows[k]
            tiles[t] = value
        w_ref[c0 : c0 + TILE, :] = jnp.where(lane <= sub + c0, top * (scale * lax.rsqrt(pivots)), 0.0)
    out_ref[...] = lax.dot_general(
        f_ref[...], w_ref[...], (((1,), (1,)), ((), ())), precision=precise, preferred_element_type=F32
    )


def ortho_call(gram_matrix, filtered, scale):
    vmem = pl.BlockSpec(memory_space=pltpu.VMEM)
    return pl.pallas_call(
        functools.partial(ortho_kernel, scale),
        name="ortho",
        out_shape=jax.ShapeDtypeStruct((BLK, VEC), F32),
        in_specs=[vmem, vmem],
        out_specs=vmem,
        scratch_shapes=[pltpu.VMEM((VEC, VEC), F32)],
    )(gram_matrix, filtered)


def per_device(start_block, inverses, iface_rows, neighbors, couplings, pole_weights):
    filtered, gram_matrix = filter_call(
        neighbors.T, pole_weights, iface_rows, couplings,
        start_block.reshape(SUB, BLK, VEC), inverses[0],
    )
    return ortho_call(gram_matrix, filtered, math.sqrt(NSUB * SUB * BLK))


def solution(mesh):
    placed = (
        P("sub", None),
        P("pole", "sub", None, None),
        P("sub", None, None),
        P("sub", None),
        P("sub", None, None),
        P("pole"),
    )
    return jax.shard_map(
        per_device, mesh=mesh, in_specs=placed, out_specs=P(("sub", "pole"), None), check_vma=False
    )
```

```python
import functools
import math

import jax
import jax.numpy as jnp
from jax import lax
from jax.experimental import pallas as pl
from jax.experimental.pallas import tpu as pltpu
from jax.sharding import PartitionSpec as P

precise = lax.Precision.HIGHEST
MESH = pl.DeviceIdType.MESH
F32 = jnp.float32
BF16 = jnp.bfloat16

SUB = 8
BLK = 512
VEC = 128
IFC = 128
PIECE = VEC // 8
EIGHT = (4, 3, 5, 2, 6, 1, 7)
FOUR = (2, 1, 3)
XROWS = 288
YROWS = BLK - XROWS
NX = 4
NSUB = 32


def pair(value):
    high = value.astype(BF16)
    low = (value - high.astype(F32)).astype(BF16)
    return jnp.concatenate([high, low], axis=1)


def fold(wide):
    return wide[:, :VEC] + wide[:, VEC:]


def mm(a, b):
    return jnp.dot(a, b, preferred_element_type=F32)


def down_lanes(row):
    return jnp.broadcast_to(row, (IFC, IFC)).T


def filter_kernel(
    nb_hbm, w_ref, rows_ref, coup_ref, start_ref, inv_ref, out_ref, gram_ref,
    nb_ref, a32, ahl, b32, outgoing, arrived, term, far_l, far_r, far_l2, far_r2, near_l, near_r, crossed, from_y, held,
    local, slot2, slot3, slot4, acc2, acc3, part,
    a_sem, b_sem, nb_sem, out_sem, ex_send, ex_recv, far_send, far_recv, near_send, near_recv,
    cross_send, cross_recv, y_send, y_recv, send2, recv2, send3, recv3, send4, recv4, send5, recv5,
):
    pole = lax.axis_index("pole")
    sub = lax.axis_index("sub")
    x = pole // 2
    yl = pole % 2
    other = 1 - yl
    yh = sub // 16
    z = (sub // 2) % 8
    core = sub % 2
    y = yh * 2 + yl
    here = x * 2 + core
    nxt = (sub + 1) % NSUB
    prv = (sub + NSUB - 1) % NSUB
    right = ((x + 1) % NX) * 2 + yl
    left = ((x + NX - 1) % NX) * 2 + yl
    across = x * 2 + other

    def at_xc(d):
        t = (here + d) % 8
        return t, ((t // 2) * 2 + yl, (yh * 8 + z) * 2 + t % 2)

    def at_y(d):
        t = (y + d) % 4
        return (x * 2 + t % 2, ((t // 2) * 8 + z) * 2 + core)

    def at_z(d):
        t = (z + d) % 8
        return (pole, (yh * 8 + t) * 2 + core)

    def fetch(s):
        return (
            pltpu.make_async_copy(inv_ref.at[s], a32.at[s], a_sem.at[s]),
            pltpu.make_async_copy(start_ref.at[s], b32.at[s], b_sem.at[s]),
        )

    fetch_nb = pltpu.make_async_copy(nb_hbm, nb_ref, nb_sem)
    for copy in fetch(0):
        copy.start()
    barrier = pltpu.get_barrier_semaphore()
    peers = [at_z(d) for d in EIGHT]
    peers += [(pole, nxt), (pole, prv)]
    peers += [at_y(d) for d in FOUR]
    peers += [at_xc(d)[1] for d in EIGHT]
    for dev in peers:
        pl.semaphore_signal(barrier, inc=1, device_id=dev, device_id_type=MESH)
    for s in range(1, SUB):
        for copy in fetch(s):
            copy.start()
    fetch_nb.start()

    def send(src, dst, s_sem, r_sem, dev):
        return pltpu.make_async_remote_copy(
            src_ref=src, dst_ref=dst, send_sem=s_sem, recv_sem=r_sem,
            device_id=dev, device_id_type=MESH,
        )

    def exchange(side, s):
        return send(
            outgoing.at[side, s], arrived.at[1 - side, s],
            ex_send.at[side, s], ex_recv.at[1 - side, s],
            (pole, prv if side == 0 else nxt),
        )

    lane_ids = lax.broadcasted_iota(jnp.int32, (IFC, BLK), 1).astype(F32)
    row_ids = lax.broadcasted_iota(jnp.int32, (BLK, 2 * IFC), 0)

    def apply(s, vectors):
        parts = pair(vectors)
        return fold(mm(ahl[s, :, :BLK], parts)) + mm(ahl[s, :, BLK:], parts[:, :VEC])

    def first(s, carry):
        for copy in fetch(s):
            copy.wait()
        a = a32[s]
        high = a.astype(BF16)
        ahl[s, :, :BLK] = high
        ahl[s, :, BLK:] = (a - high.astype(F32)).astype(BF16)
        parts = pair(apply(s, b32[s]))
        rows = rows_ref[s].astype(F32)
        for side in range(2):
            ids = down_lanes(rows[side : side + 1])
            pick = (lane_ids == jnp.concatenate([ids] * (BLK // IFC), axis=1)).astype(F32).astype(BF16)
            outgoing[side, s] = fold(mm(pick, parts))

        @pl.when(s == 0)
        def _():
            pl.semaphore_wait(barrier, len(peers))

        for side in range(2):
            exchange(side, s).start()
        return carry

    lax.fori_loop(0, SUB, first, 0)
    fetch_nb.wait()

    def arrive(s, carry):
        exchange(0, s).wait()
        exchange(1, s).wait()
        return carry

    lax.fori_loop(0, SUB, arrive, 0)

    weight = w_ref[0]

    def second(s):
        rows = rows_ref[s]
        coup = coup_ref[s]
        low = arrived[0, lax.rem(nb_ref[0, s], SUB)] * down_lanes(coup[0:1])
        high = arrived[1, lax.rem(nb_ref[1, s], SUB)] * down_lanes(coup[1:2])
        terms = pair(jnp.concatenate([low, high], axis=0))
        row = jnp.concatenate([rows[0:1], rows[1:2]], axis=1)
        place = (row_ids == row).astype(F32).astype(BF16)
        term[s] = weight * apply(s, b32[s] + fold(mm(place, terms)))

    def owner(shift, kind):
        return ((x + shift) % NX) * 2 + (other if kind == 0 else yl)

    lo, hi = pl.ds(0, XROWS // 2), pl.ds(XROWS // 2, XROWS // 2)
    ylo, yhi = pl.ds(XROWS, YROWS // 2), pl.ds(XROWS + YROWS // 2, YROWS // 2)
    xrows, yrows = pl.ds(0, XROWS), pl.ds(XROWS, YROWS)

    def far(kind):
        s = owner(2, min(kind, 1))
        to_r, to_l = (lo, hi) if kind < 2 else (ylo, yhi)
        dst_r = far_l.at[kind] if kind < 2 else far_l2
        dst_l = far_r.at[kind] if kind < 2 else far_r2
        return (
            send(term.at[s, to_r], dst_r, far_send.at[0, kind], far_recv.at[0, kind], (right, sub)),
            send(term.at[s, to_l], dst_l, far_send.at[1, kind], far_recv.at[1, kind], (left, sub)),
        )

    def near(kind, step):
        low, high = (lo, hi) if kind < 2 else (ylo, yhi)
        to_r, to_l = (high, low) if step == 0 else (low, high)
        s, slot = min(kind, 1), min(kind, 1)
        return (
            send(term.at[owner(1, s), to_r], near_l.at[slot, to_r], near_send.at[0, kind, step],
                 near_recv.at[0, kind, step], (right, sub)),
            send(term.at[owner(3, s), to_l], near_r.at[slot, to_l], near_send.at[1, kind, step],
                 near_recv.at[1, kind, step], (left, sub)),
        )

    def cross(shift):
        return send(
            term.at[owner(shift, 0), yrows], crossed.at[shift],
            cross_send.at[shift], cross_recv.at[shift], (across, sub),
        )

    def relay(kind):
        far_a, far_b = far(kind)
        low, high = (lo, hi) if kind < 2 else (ylo, yhi)
        s = owner(1, min(kind, 1))
        far_a.wait_recv()
        term[s, low] = term[s, low] + (far_l[kind] if kind < 2 else far_l2[...])
        near(kind, 1)[0].start()
        s = owner(3, min(kind, 1))
        far_b.wait_recv()
        term[s, high] = term[s, high] + (far_r[kind] if kind < 2 else far_r2[...])
        near(kind, 1)[1].start()

    def join(shift):
        cross(shift).wait_recv()
        s = owner(shift, 1)
        term[s, yrows] = term[s, yrows] + crossed[shift]

    def sequence(i, carry):
        shift = jnp.where(i < 2, 2, jnp.where(i < 5, (2 * i - 3) % 4, (2 * i - 9) % 4))
        shift = jnp.where((i == 4) | (i == 7), 0, shift)
        kind = jnp.where((i == 1) | (i > 4), 1, 0)

        @pl.when(i == 7)
        def _():
            relay(0)

        second(((x + shift) % NX) * 2 + jnp.where(kind == 0, other, yl))

        @pl.when(i == 0)
        def _():
            far(0)[0].start()
            far(0)[1].start()
            cross(2).start()

        @pl.when(i == 1)
        def _():
            far(1)[0].start()
            far(1)[1].start()

        @pl.when(i == 2)
        def _():
            near(0, 0)[0].start()
            cross(1).start()

        @pl.when(i == 3)
        def _():
            near(0, 0)[1].start()
            cross(3).start()

        @pl.when(i == 4)
        def _():
            cross(0).start()
        return carry

    lax.fori_loop(0, SUB, sequence, 0)

    join(2)
    for copy in far(2) + near(1, 0):
        copy.start()
    relay(1)
    join(1)
    near(2, 0)[0].start()
    join(3)
    near(2, 0)[1].start()

    own = owner(0, 0)
    for copy in near(0, 0) + near(0, 1):
        copy.wait_recv()
    term[own, xrows] = term[own, xrows] + near_l[0, xrows] + near_r[0, xrows]
    hand = send(term.at[own, xrows], from_y, y_send, y_recv, (across, sub))
    hand.start()
    relay(2)
    join(0)
    for copy in near(1, 0) + near(1, 1) + near(2, 0) + near(2, 1):
        copy.wait_recv()
    own = owner(0, 1)
    hand.wait_recv()
    term[own, xrows] = term[own, xrows] + from_y[...]
    mine = term[own] + near_l[1] + near_r[1]
    held[...] = mine
    leave = pltpu.make_async_copy(held, out_ref, out_sem)
    leave.start()

    parts = pair(mine)
    four = lax.dot_general(parts, parts, (((0,), (0,)), ((), ())), preferred_element_type=F32)
    local[...] = fold(four[:VEC]) + fold(four[VEC:])

    def rows_of(n):
        return pl.ds(pl.multiple_of(n * PIECE, PIECE), PIECE)

    copies2 = []
    for d in range(1, 8):
        t, dev = at_xc(d)
        copies2.append(send(local.at[rows_of(t)], slot2.at[d - 1], send2.at[d - 1], recv2.at[d - 1], dev))
    for d in EIGHT:
        copies2[d - 1].start()
    total = local[rows_of(here)]
    for d in range(7):
        copies2[d].wait_recv()
        total = total + slot2[d]
    acc2[...] = total

    copies3 = [
        send(acc2, slot3.at[d - 1], send3.at[d - 1], recv3.at[d - 1], at_y(d)) for d in range(1, 4)
    ]
    for d in FOUR:
        copies3[d - 1].start()
    for d in range(3):
        copies3[d].wait_recv()
        total = total + slot3[d]
    acc3[...] = total

    copies4 = [
        send(acc3, slot4.at[d - 1], send4.at[d - 1], recv4.at[d - 1], at_z(d)) for d in range(1, 8)
    ]
    for d in EIGHT:
        copies4[d - 1].start()
    for d in range(7):
        copies4[d].wait_recv()
        total = total + slot4[d]
    part[...] = total
    gram_ref[rows_of(here)] = total

    copies5 = [
        send(part, gram_ref.at[rows_of(here)], send5.at[d - 1], recv5.at[d - 1], at_xc(d)[1])
        for d in range(1, 8)
    ]
    for d in EIGHT:
        copies5[d - 1].start()
    hand.wait_send()
    for kind in range(3):
        for copy in far(kind) + near(kind, 0) + near(kind, 1):
            copy.wait_send()
    for shift in range(NX):
        cross(shift).wait_send()
    for copy in copies2 + copies3 + copies4:
        copy.wait_send()
    leave.wait()
    for copy in copies5:
        copy.wait()


def filter_call(neighbors, pole_weights, iface_rows, couplings, start, inverses):
    dma = pltpu.SemaphoreType.DMA
    vmem = pl.BlockSpec(memory_space=pltpu.VMEM)
    smem = pl.BlockSpec(memory_space=pltpu.SMEM)
    hbm = pl.BlockSpec(memory_space=pl.ANY)
    return pl.pallas_call(
        filter_kernel,
        name="filter_pass",
        out_shape=(
            jax.ShapeDtypeStruct((BLK, VEC), F32),
            jax.ShapeDtypeStruct((VEC, VEC), F32),
        ),
        in_specs=[hbm, smem, vmem, vmem, hbm, hbm],
        out_specs=(hbm, vmem),
        scratch_shapes=[
            pltpu.SMEM((2, SUB), jnp.int32),
            pltpu.VMEM((SUB, BLK, BLK), F32),
            pltpu.VMEM((SUB, BLK, 2 * BLK), BF16),
            pltpu.VMEM((SUB, BLK, VEC), F32),
            pltpu.VMEM((2, SUB, IFC, VEC), F32),
            pltpu.VMEM((2, SUB, IFC, VEC), F32),
            pltpu.VMEM((SUB, BLK, VEC), F32),
            pltpu.VMEM((2, XROWS // 2, VEC), F32),
            pltpu.VMEM((2, XROWS // 2, VEC), F32),
            pltpu.VMEM((YROWS // 2, VEC), F32),
            pltpu.VMEM((YROWS // 2, VEC), F32),
            pltpu.VMEM((2, BLK, VEC), F32),
            pltpu.VMEM((2, BLK, VEC), F32),
            pltpu.VMEM((NX, YROWS, VEC), F32),
            pltpu.VMEM((XROWS, VEC), F32),
            pltpu.VMEM((BLK, VEC), F32),
            pltpu.VMEM((VEC, VEC), F32),
            pltpu.VMEM((7, PIECE, VEC), F32),
            pltpu.VMEM((3, PIECE, VEC), F32),
            pltpu.VMEM((7, PIECE, VEC), F32),
            pltpu.VMEM((PIECE, VEC), F32),
            pltpu.VMEM((PIECE, VEC), F32),
            pltpu.VMEM((PIECE, VEC), F32),
            dma((SUB,)), dma((SUB,)), dma, dma,
            dma((2, SUB)), dma((2, SUB)),
            dma((2, 3)), dma((2, 3)),
            dma((2, 3, 2)), dma((2, 3, 2)),
            dma((NX,)), dma((NX,)), dma, dma,
            dma((7,)), dma((7,)), dma((3,)), dma((3,)),
            dma((7,)), dma((7,)), dma((7,)), dma((7,)),
        ],
        compiler_params=pltpu.CompilerParams(
            collective_id=0, has_side_effects=True, vmem_limit_bytes=56 * 1024 * 1024
        ),
    )(neighbors, pole_weights, iface_rows, couplings, start, inverses)


TILE = 8
PANEL = 16
CLOSE = 2


def spread(row):
    return jnp.broadcast_to(row, (TILE, VEC))


def three(value):
    first = value.astype(BF16)
    rest = value - first.astype(F32)
    second = rest.astype(BF16)
    return first, second, (rest - second.astype(F32)).astype(BF16)


def six_terms(a, b, axis):
    a1, a2, a3 = three(a)
    b1, b2, b3 = three(b)
    return (
        jnp.concatenate([a1, a1, a2, a1, a3, a2], axis=axis),
        jnp.concatenate([b1, b2, b1, b3, b1, b2], axis=axis),
    )


def ortho_kernel(scale, g_ref, f_ref, out_ref, w_ref):
    count, tall = VEC // TILE, PANEL // TILE
    tiles = [g_ref[TILE * t : TILE * t + TILE, :] for t in range(count)]
    sub = lax.broadcasted_iota(jnp.int32, (TILE, VEC), 0)
    lane = lax.broadcasted_iota(jnp.int32, (TILE, VEC), 1)
    below = [(sub > k).astype(F32) for k in range(TILE)]
    for p in range(0, count, tall):
        c0 = TILE * p
        own = list(range(p, p + tall))
        close = list(range(p + tall, min(count, p + tall + CLOSE)))
        cols = {
            (m, t): jnp.broadcast_to(tiles[t][:, c0 + m : c0 + m + 1], (TILE, VEC))
            for t in own + close
            for m in range(PANEL)
        }
        panel = (lane >= c0) & (lane < c0 + PANEL)
        top = {t: jnp.where(panel, (lane == sub + TILE * t).astype(F32), tiles[t]) for t in own}
        pivots = {t: jnp.ones((TILE, VEC), F32) for t in own}
        inverses = dict(pivots)
        factors, rows = {}, []
        for k in range(PANEL):
            t0, r = p + k // TILE, k % TILE
            pivot = spread(cols[k, t0][r : r + 1])
            inverse = 1.0 / pivot
            pivots[t0] = jnp.where(sub == r, pivot, pivots[t0])
            inverses[t0] = jnp.where(sub == r, inverse, inverses[t0])
            upper = {m: spread(cols[m, t0][r : r + 1]) for m in range(k + 1, PANEL)}
            row = spread(top[t0][r : r + 1])
            rows.append(row)
            for t in range(t0, p + tall):
                for m in range(k + 1, PANEL):
                    cols[m, t] = cols[m, t] - (cols[k, t] * upper[m]) * inverse
                column = cols[k, t] * below[r] if t == t0 else cols[k, t]
                top[t] = top[t] - (column * row) * inverse
            for t in close:
                f = cols[k, t] * inverse
                factors[k, t] = f
                for m in range(k + 1, PANEL):
                    cols[m, t] = cols[m, t] - f * upper[m]
        for t in close:
            terms = [factors[k, t] * rows[k] for k in range(PANEL)]
            while len(terms) > 1:
                terms = [terms[i] + terms[i + 1] for i in range(0, len(terms), 2)]
            tiles[t] = jnp.where(panel, 0.0, tiles[t]) - terms[0]
        distant = p + tall + CLOSE
        if distant < count:
            final = jnp.concatenate([top[t] for t in own], axis=0)
            a, b = six_terms(final * jnp.concatenate([inverses[t] for t in own], axis=0), final, 0)
            update = lax.dot_general(a, b, (((0,), (0,)), ((), ())), preferred_element_type=F32)
            for t in range(distant, count):
                tiles[t] = jnp.where(panel, 0.0, tiles[t]) - update[TILE * t : TILE * t + TILE]
        for t in own:
            w_ref[TILE * t : TILE * t + TILE, :] = jnp.where(
                lane <= sub + TILE * t, top[t] * (scale * lax.rsqrt(pivots[t])), 0.0
            )
    a1, a2, a3 = three(f_ref[...])
    b1, b2, b3 = three(w_ref[...])
    along = (((1,), (1,)), ((), ()))
    wide = lax.dot_general(
        jnp.concatenate([a1, a2], axis=1),
        jnp.concatenate([jnp.concatenate([b1, b1], axis=1), jnp.concatenate([b2, b2], axis=1)], axis=0),
        along, preferred_element_type=F32,
    )
    small = lax.dot_general(
        jnp.concatenate([a1, a3], axis=1), jnp.concatenate([b3, b1], axis=1),
        along, preferred_element_type=F32,
    )
    out_ref[...] = wide[:, :VEC] + (wide[:, VEC:] + small)


def ortho_call(gram_matrix, filtered, scale):
    vmem = pl.BlockSpec(memory_space=pltpu.VMEM)
    return pl.pallas_call(
        functools.partial(ortho_kernel, scale),
        name="ortho",
        out_shape=jax.ShapeDtypeStruct((BLK, VEC), F32),
        in_specs=[vmem, vmem],
        out_specs=vmem,
        scratch_shapes=[pltpu.VMEM((VEC, VEC), F32)],
    )(gram_matrix, filtered)


def per_device(start_block, inverses, iface_rows, neighbors, couplings, pole_weights):
    filtered, gram_matrix = filter_call(
        neighbors.T, pole_weights, iface_rows, couplings,
        start_block.reshape(SUB, BLK, VEC), inverses[0],
    )
    return ortho_call(gram_matrix, filtered, math.sqrt(NSUB * SUB * BLK))


def solution(mesh):
    placed = (
        P("sub", None),
        P("pole", "sub", None, None),
        P("sub", None, None),
        P("sub", None),
        P("sub", None, None),
        P("pole"),
    )
    return jax.shard_map(
        per_device, mesh=mesh, in_specs=placed, out_specs=P(("sub", "pole"), None), check_vma=False
    )
```

```python
import functools
import math

import jax
import jax.numpy as jnp
from jax import lax
from jax.experimental import pallas as pl
from jax.experimental.pallas import tpu as pltpu
from jax.sharding import PartitionSpec as P

precise = lax.Precision.HIGHEST
MESH = pl.DeviceIdType.MESH
F32 = jnp.float32
BF16 = jnp.bfloat16

SUB = 8
BLK = 512
VEC = 128
IFC = 128
PIECE = VEC // 8
EIGHT = (4, 3, 5, 2, 6, 1, 7)
FOUR = (2, 1, 3)
XROWS = 288
YROWS = BLK - XROWS
NX = 4
NSUB = 32


def pair(value):
    high = value.astype(BF16)
    low = (value - high.astype(F32)).astype(BF16)
    return jnp.concatenate([high, low], axis=1)


def fold(wide):
    return wide[:, :VEC] + wide[:, VEC:]


def mm(a, b):
    return jnp.dot(a, b, preferred_element_type=F32)


def down_lanes(row):
    return jnp.broadcast_to(row, (IFC, IFC)).T


def filter_kernel(
    nb_hbm, w_hbm, rows_hbm, coup_hbm, start_ref, inv_ref, out_ref, gram_ref,
    nb_ref, w_ref, rows_ref, coup_ref, a32, ahl, b32, outgoing, arrived, term, far_l, far_r, far_l2, far_r2, near_l, near_r, crossed, from_y, held,
    local, slot2, slot3, slot4, acc2, acc3, part,
    round_sem, a_sem, b_sem, small_sem, out_sem, ex_send, ex_recv, far_send, far_recv, near_send, near_recv,
    cross_send, cross_recv, y_send, y_recv, send2, recv2, send3, recv3, send4, recv4, send5, recv5,
):
    pole = lax.axis_index("pole")
    sub = lax.axis_index("sub")
    x = pole // 2
    yl = pole % 2
    other = 1 - yl
    yh = sub // 16
    z = (sub // 2) % 8
    core = sub % 2
    y = yh * 2 + yl
    here = x * 2 + core
    nxt = (sub + 1) % NSUB
    prv = (sub + NSUB - 1) % NSUB
    right = ((x + 1) % NX) * 2 + yl
    left = ((x + NX - 1) % NX) * 2 + yl
    across = x * 2 + other

    def at_xc(d):
        t = (here + d) % 8
        return t, ((t // 2) * 2 + yl, (yh * 8 + z) * 2 + t % 2)

    def at_y(d):
        t = (y + d) % 4
        return (x * 2 + t % 2, ((t // 2) * 8 + z) * 2 + core)

    def at_z(d):
        t = (z + d) % 8
        return (pole, (yh * 8 + t) * 2 + core)

    def fetch(s):
        return (
            pltpu.make_async_copy(inv_ref.at[s], a32.at[s], a_sem.at[s]),
            pltpu.make_async_copy(start_ref.at[s], b32.at[s], b_sem.at[s]),
        )

    small = [
        pltpu.make_async_copy(src, dst, small_sem.at[i])
        for i, (src, dst) in enumerate(
            ((rows_hbm, rows_ref), (coup_hbm, coup_ref), (nb_hbm, nb_ref), (w_hbm, w_ref))
        )
    ]
    for copy in fetch(0):
        copy.start()
    for copy in small:
        copy.start()
    barrier = pltpu.get_barrier_semaphore()
    z_near = (at_z(1), at_z(7))
    peers = [(pole, nxt), (pole, prv), *z_near, at_y(1), at_y(3), (right, sub), (left, sub)]
    for dev in peers:
        pl.semaphore_signal(barrier, inc=1, device_id=dev, device_id_type=MESH)
    for s in range(1, SUB):
        for copy in fetch(s):
            copy.start()

    def tell(n):
        for dev in z_near:
            pl.semaphore_signal(round_sem.at[n], inc=1, device_id=dev, device_id_type=MESH)

    def hear(n):
        pl.semaphore_wait(round_sem.at[n], 2)

    def send(src, dst, s_sem, r_sem, dev):
        return pltpu.make_async_remote_copy(
            src_ref=src, dst_ref=dst, send_sem=s_sem, recv_sem=r_sem,
            device_id=dev, device_id_type=MESH,
        )

    def exchange(side, s):
        return send(
            outgoing.at[side, s], arrived.at[1 - side, s],
            ex_send.at[side, s], ex_recv.at[1 - side, s],
            (pole, prv if side == 0 else nxt),
        )

    lane_ids = lax.broadcasted_iota(jnp.int32, (IFC, BLK), 1).astype(F32)
    row_ids = lax.broadcasted_iota(jnp.int32, (BLK, 2 * IFC), 0)

    def apply(s, vectors):
        parts = pair(vectors)
        return fold(mm(ahl[s, :, :BLK], parts)) + mm(ahl[s, :, BLK:], parts[:, :VEC])

    def first(s, carry):
        for copy in fetch(s):
            copy.wait()
        a = a32[s]
        high = a.astype(BF16)
        ahl[s, :, :BLK] = high
        ahl[s, :, BLK:] = (a - high.astype(F32)).astype(BF16)
        parts = pair(apply(s, b32[s]))
        rows = rows_ref[s].astype(F32)
        for side in range(2):
            ids = down_lanes(rows[side : side + 1])
            pick = (lane_ids == jnp.concatenate([ids] * (BLK // IFC), axis=1)).astype(F32).astype(BF16)
            outgoing[side, s] = fold(mm(pick, parts))

        @pl.when(s == 0)
        def _():
            pl.semaphore_wait(barrier, len(peers))
            tell(0)

        for side in range(2):
            exchange(side, s).start()
        return carry

    for copy in small:
        copy.wait()
    lax.fori_loop(0, SUB, first, 0)
    hear(0)
    tell(1)

    def arrive(s, carry):
        exchange(0, s).wait()
        exchange(1, s).wait()
        return carry

    lax.fori_loop(0, SUB, arrive, 0)

    weight = w_ref[0]

    def second(s):
        rows = rows_ref[s]
        coup = coup_ref[s]
        low = arrived[0, lax.rem(nb_ref[0, s], SUB)] * down_lanes(coup[0:1])
        high = arrived[1, lax.rem(nb_ref[1, s], SUB)] * down_lanes(coup[1:2])
        terms = pair(jnp.concatenate([low, high], axis=0))
        row = jnp.concatenate([rows[0:1], rows[1:2]], axis=1)
        place = (row_ids == row).astype(F32).astype(BF16)
        term[s] = weight * apply(s, b32[s] + fold(mm(place, terms)))

    def owner(shift, kind):
        return ((x + shift) % NX) * 2 + (other if kind == 0 else yl)

    lo, hi = pl.ds(0, XROWS // 2), pl.ds(XROWS // 2, XROWS // 2)
    ylo, yhi = pl.ds(XROWS, YROWS // 2), pl.ds(XROWS + YROWS // 2, YROWS // 2)
    xrows, yrows = pl.ds(0, XROWS), pl.ds(XROWS, YROWS)

    def far(kind):
        s = owner(2, min(kind, 1))
        to_r, to_l = (lo, hi) if kind < 2 else (ylo, yhi)
        dst_r = far_l.at[kind] if kind < 2 else far_l2
        dst_l = far_r.at[kind] if kind < 2 else far_r2
        return (
            send(term.at[s, to_r], dst_r, far_send.at[0, kind], far_recv.at[0, kind], (right, sub)),
            send(term.at[s, to_l], dst_l, far_send.at[1, kind], far_recv.at[1, kind], (left, sub)),
        )

    def near(kind, step):
        low, high = (lo, hi) if kind < 2 else (ylo, yhi)
        to_r, to_l = (high, low) if step == 0 else (low, high)
        s, slot = min(kind, 1), min(kind, 1)
        return (
            send(term.at[owner(1, s), to_r], near_l.at[slot, to_r], near_send.at[0, kind, step],
                 near_recv.at[0, kind, step], (right, sub)),
            send(term.at[owner(3, s), to_l], near_r.at[slot, to_l], near_send.at[1, kind, step],
                 near_recv.at[1, kind, step], (left, sub)),
        )

    def cross(shift):
        return send(
            term.at[owner(shift, 0), yrows], crossed.at[shift],
            cross_send.at[shift], cross_recv.at[shift], (across, sub),
        )

    def relay(kind):
        far_a, far_b = far(kind)
        low, high = (lo, hi) if kind < 2 else (ylo, yhi)
        s = owner(1, min(kind, 1))
        far_a.wait_recv()
        term[s, low] = term[s, low] + (far_l[kind] if kind < 2 else far_l2[...])
        near(kind, 1)[0].start()
        s = owner(3, min(kind, 1))
        far_b.wait_recv()
        term[s, high] = term[s, high] + (far_r[kind] if kind < 2 else far_r2[...])
        near(kind, 1)[1].start()

    def join(shift):
        cross(shift).wait_recv()
        s = owner(shift, 1)
        term[s, yrows] = term[s, yrows] + crossed[shift]

    def sequence(i, carry):
        shift = jnp.where(i < 2, 2, jnp.where(i < 5, (2 * i - 3) % 4, (2 * i - 9) % 4))
        shift = jnp.where((i == 4) | (i == 7), 0, shift)
        kind = jnp.where((i == 1) | (i > 4), 1, 0)

        @pl.when(i == 7)
        def _():
            relay(0)

        second(((x + shift) % NX) * 2 + jnp.where(kind == 0, other, yl))

        @pl.when(i == 0)
        def _():
            far(0)[0].start()
            far(0)[1].start()
            cross(2).start()

        @pl.when(i == 1)
        def _():
            far(1)[0].start()
            far(1)[1].start()

        @pl.when(i == 2)
        def _():
            near(0, 0)[0].start()
            cross(1).start()

        @pl.when(i == 3)
        def _():
            near(0, 0)[1].start()
            cross(3).start()

        @pl.when(i == 4)
        def _():
            cross(0).start()
        return carry

    lax.fori_loop(0, SUB, sequence, 0)
    hear(1)
    tell(2)

    join(2)
    for copy in far(2) + near(1, 0):
        copy.start()
    relay(1)
    join(1)
    near(2, 0)[0].start()
    join(3)
    near(2, 0)[1].start()

    own = owner(0, 0)
    for copy in near(0, 0) + near(0, 1):
        copy.wait_recv()
    term[own, xrows] = term[own, xrows] + near_l[0, xrows] + near_r[0, xrows]
    hand = send(term.at[own, xrows], from_y, y_send, y_recv, (across, sub))
    hand.start()
    relay(2)
    join(0)
    for copy in near(1, 0) + near(1, 1) + near(2, 0) + near(2, 1):
        copy.wait_recv()
    own = owner(0, 1)
    hand.wait_recv()
    term[own, xrows] = term[own, xrows] + from_y[...]
    mine = term[own] + near_l[1] + near_r[1]
    held[...] = mine
    leave = pltpu.make_async_copy(held, out_ref, out_sem)
    leave.start()
    hear(2)

    parts = pair(mine)
    four = lax.dot_general(parts, parts, (((0,), (0,)), ((), ())), preferred_element_type=F32)
    local[...] = fold(four[:VEC]) + fold(four[VEC:])

    def rows_of(n):
        return pl.ds(pl.multiple_of(n * PIECE, PIECE), PIECE)

    copies2 = []
    for d in range(1, 8):
        t, dev = at_xc(d)
        copies2.append(send(local.at[rows_of(t)], slot2.at[d - 1], send2.at[d - 1], recv2.at[d - 1], dev))
    for d in EIGHT:
        copies2[d - 1].start()
    total = local[rows_of(here)]
    for d in range(7):
        copies2[d].wait_recv()
        total = total + slot2[d]
    acc2[...] = total

    copies3 = [
        send(acc2, slot3.at[d - 1], send3.at[d - 1], recv3.at[d - 1], at_y(d)) for d in range(1, 4)
    ]
    for d in FOUR:
        copies3[d - 1].start()
    for d in range(3):
        copies3[d].wait_recv()
        total = total + slot3[d]
    acc3[...] = total

    copies4 = [
        send(acc3, slot4.at[d - 1], send4.at[d - 1], recv4.at[d - 1], at_z(d)) for d in range(1, 8)
    ]
    for d in EIGHT:
        copies4[d - 1].start()
    for d in range(7):
        copies4[d].wait_recv()
        total = total + slot4[d]
    part[...] = total
    gram_ref[rows_of(here)] = total

    copies5 = [
        send(part, gram_ref.at[rows_of(here)], send5.at[d - 1], recv5.at[d - 1], at_xc(d)[1])
        for d in range(1, 8)
    ]
    for d in EIGHT:
        copies5[d - 1].start()
    hand.wait_send()
    for kind in range(3):
        for copy in far(kind) + near(kind, 0) + near(kind, 1):
            copy.wait_send()
    for shift in range(NX):
        cross(shift).wait_send()
    for copy in copies2 + copies3 + copies4:
        copy.wait_send()
    leave.wait()
    for copy in copies5:
        copy.wait()


def filter_call(neighbors, pole_weights, iface_rows, couplings, start, inverses):
    dma = pltpu.SemaphoreType.DMA
    vmem = pl.BlockSpec(memory_space=pltpu.VMEM)
    hbm = pl.BlockSpec(memory_space=pltpu.HBM)
    return pl.pallas_call(
        filter_kernel,
        name="filter_pass",
        out_shape=(
            jax.ShapeDtypeStruct((BLK, VEC), F32),
            jax.ShapeDtypeStruct((VEC, VEC), F32),
        ),
        in_specs=[hbm] * 6,
        out_specs=(hbm, vmem),
        scratch_shapes=[
            pltpu.SMEM((2, SUB), jnp.int32),
            pltpu.SMEM((1,), F32),
            pltpu.VMEM((SUB, 2, IFC), jnp.int32),
            pltpu.VMEM((SUB, 2, IFC), F32),
            pltpu.VMEM((SUB, BLK, BLK), F32),
            pltpu.VMEM((SUB, BLK, 2 * BLK), BF16),
            pltpu.VMEM((SUB, BLK, VEC), F32),
            pltpu.VMEM((2, SUB, IFC, VEC), F32),
            pltpu.VMEM((2, SUB, IFC, VEC), F32),
            pltpu.VMEM((SUB, BLK, VEC), F32),
            pltpu.VMEM((2, XROWS // 2, VEC), F32),
            pltpu.VMEM((2, XROWS // 2, VEC), F32),
            pltpu.VMEM((YROWS // 2, VEC), F32),
            pltpu.VMEM((YROWS // 2, VEC), F32),
            pltpu.VMEM((2, BLK, VEC), F32),
            pltpu.VMEM((2, BLK, VEC), F32),
            pltpu.VMEM((NX, YROWS, VEC), F32),
            pltpu.VMEM((XROWS, VEC), F32),
            pltpu.VMEM((BLK, VEC), F32),
            pltpu.VMEM((VEC, VEC), F32),
            pltpu.VMEM((7, PIECE, VEC), F32),
            pltpu.VMEM((3, PIECE, VEC), F32),
            pltpu.VMEM((7, PIECE, VEC), F32),
            pltpu.VMEM((PIECE, VEC), F32),
            pltpu.VMEM((PIECE, VEC), F32),
            pltpu.VMEM((PIECE, VEC), F32),
            pltpu.SemaphoreType.REGULAR((3,)),
            dma((SUB,)), dma((SUB,)), dma((4,)), dma,
            dma((2, SUB)), dma((2, SUB)),
            dma((2, 3)), dma((2, 3)),
            dma((2, 3, 2)), dma((2, 3, 2)),
            dma((NX,)), dma((NX,)), dma, dma,
            dma((7,)), dma((7,)), dma((3,)), dma((3,)),
            dma((7,)), dma((7,)), dma((7,)), dma((7,)),
        ],
        compiler_params=pltpu.CompilerParams(
            collective_id=0, has_side_effects=True, vmem_limit_bytes=56 * 1024 * 1024
        ),
    )(neighbors, pole_weights, iface_rows, couplings, start, inverses)


TILE = 8
PANEL = 16
CLOSE = 2


def spread(row):
    return jnp.broadcast_to(row, (TILE, VEC))


def three(value):
    first = value.astype(BF16)
    rest = value - first.astype(F32)
    second = rest.astype(BF16)
    return first, second, (rest - second.astype(F32)).astype(BF16)


def six_terms(a, b, axis):
    a1, a2, a3 = three(a)
    b1, b2, b3 = three(b)
    return (
        jnp.concatenate([a1, a1, a2, a1, a3, a2], axis=axis),
        jnp.concatenate([b1, b2, b1, b3, b1, b2], axis=axis),
    )


def ortho_kernel(scale, g_ref, f_ref, out_ref, w_ref):
    count, tall = VEC // TILE, PANEL // TILE
    tiles = [g_ref[TILE * t : TILE * t + TILE, :] for t in range(count)]
    sub = lax.broadcasted_iota(jnp.int32, (TILE, VEC), 0)
    lane = lax.broadcasted_iota(jnp.int32, (TILE, VEC), 1)
    below = [(sub > k).astype(F32) for k in range(TILE)]
    for p in range(0, count, tall):
        c0 = TILE * p
        own = list(range(p, p + tall))
        close = list(range(p + tall, min(count, p + tall + CLOSE)))
        cols = {
            (m, t): jnp.broadcast_to(tiles[t][:, c0 + m : c0 + m + 1], (TILE, VEC))
            for t in own + close
            for m in range(PANEL)
        }
        panel = (lane >= c0) & (lane < c0 + PANEL)
        top = {t: jnp.where(panel, (lane == sub + TILE * t).astype(F32), tiles[t]) for t in own}
        pivots = {t: jnp.ones((TILE, VEC), F32) for t in own}
        inverses = dict(pivots)
        factors, rows = {}, []
        for k in range(PANEL):
            t0, r = p + k // TILE, k % TILE
            pivot = spread(cols[k, t0][r : r + 1])
            inverse = 1.0 / pivot
            pivots[t0] = jnp.where(sub == r, pivot, pivots[t0])
            inverses[t0] = jnp.where(sub == r, inverse, inverses[t0])
            upper = {m: spread(cols[m, t0][r : r + 1]) for m in range(k + 1, PANEL)}
            row = spread(top[t0][r : r + 1])
            rows.append(row)
            for t in range(t0, p + tall):
                for m in range(k + 1, PANEL):
                    cols[m, t] = cols[m, t] - (cols[k, t] * upper[m]) * inverse
                column = cols[k, t] * below[r] if t == t0 else cols[k, t]
                top[t] = top[t] - (column * row) * inverse
            for t in close:
                f = cols[k, t] * inverse
                factors[k, t] = f
                for m in range(k + 1, PANEL):
                    cols[m, t] = cols[m, t] - f * upper[m]
        for t in close:
            terms = [factors[k, t] * rows[k] for k in range(PANEL)]
            while len(terms) > 1:
                terms = [terms[i] + terms[i + 1] for i in range(0, len(terms), 2)]
            tiles[t] = jnp.where(panel, 0.0, tiles[t]) - terms[0]
        distant = p + tall + CLOSE
        if distant < count:
            final = jnp.concatenate([top[t] for t in own], axis=0)
            a, b = six_terms(final * jnp.concatenate([inverses[t] for t in own], axis=0), final, 0)
            update = lax.dot_general(a, b, (((0,), (0,)), ((), ())), preferred_element_type=F32)
            for t in range(distant, count):
                tiles[t] = jnp.where(panel, 0.0, tiles[t]) - update[TILE * t : TILE * t + TILE]
        for t in own:
            w_ref[TILE * t : TILE * t + TILE, :] = jnp.where(
                lane <= sub + TILE * t, top[t] * (scale * lax.rsqrt(pivots[t])), 0.0
            )
    a1, a2, a3 = three(f_ref[...])
    b1, b2, b3 = three(w_ref[...])
    along = (((1,), (1,)), ((), ()))
    wide = lax.dot_general(
        jnp.concatenate([a1, a2], axis=1),
        jnp.concatenate([jnp.concatenate([b1, b1], axis=1), jnp.concatenate([b2, b2], axis=1)], axis=0),
        along, preferred_element_type=F32,
    )
    small = lax.dot_general(
        jnp.concatenate([a1, a3], axis=1), jnp.concatenate([b3, b1], axis=1),
        along, preferred_element_type=F32,
    )
    out_ref[...] = wide[:, :VEC] + (wide[:, VEC:] + small)


def ortho_call(gram_matrix, filtered, scale):
    vmem = pl.BlockSpec(memory_space=pltpu.VMEM)
    return pl.pallas_call(
        functools.partial(ortho_kernel, scale),
        name="ortho",
        out_shape=jax.ShapeDtypeStruct((BLK, VEC), F32),
        in_specs=[vmem, vmem],
        out_specs=vmem,
        scratch_shapes=[pltpu.VMEM((VEC, VEC), F32)],
    )(gram_matrix, filtered)


def per_device(start_block, inverses, iface_rows, neighbors, couplings, pole_weights):
    filtered, gram_matrix = filter_call(
        neighbors.T, pole_weights, iface_rows, couplings,
        start_block.reshape(SUB, BLK, VEC), inverses[0],
    )
    return ortho_call(gram_matrix, filtered, math.sqrt(NSUB * SUB * BLK))


def solution(mesh):
    placed = (
        P("sub", None),
        P("pole", "sub", None, None),
        P("sub", None, None),
        P("sub", None),
        P("sub", None, None),
        P("pole"),
    )
    return jax.shard_map(
        per_device, mesh=mesh, in_specs=placed, out_specs=P(("sub", "pole"), None), check_vma=False
    )
```

```python
import functools
import math

import jax
import jax.numpy as jnp
from jax import lax
from jax.experimental import pallas as pl
from jax.experimental.pallas import tpu as pltpu
from jax.sharding import PartitionSpec as P

precise = lax.Precision.HIGHEST
MESH = pl.DeviceIdType.MESH
F32 = jnp.float32
BF16 = jnp.bfloat16

SUB = 8
BLK = 512
VEC = 128
IFC = 128
PIECE = VEC // 8
EIGHT = (4, 3, 5, 2, 6, 1, 7)
FOUR = (2, 1, 3)
XROWS = 288
YROWS = BLK - XROWS
NX = 4
NSUB = 32


def pair(value):
    high = value.astype(BF16)
    low = (value - high.astype(F32)).astype(BF16)
    return jnp.concatenate([high, low], axis=1)


def fold(wide):
    return wide[:, :VEC] + wide[:, VEC:]


def mm(a, b):
    return jnp.dot(a, b, preferred_element_type=F32)


def down_lanes(row):
    return jnp.broadcast_to(row, (IFC, IFC)).T


def filter_kernel(
    nb_hbm, w_hbm, rows_hbm, coup_hbm, start_ref, inv_ref, out_ref, gram_ref,
    nb_ref, w_ref, rows_ref, coup_ref, a32, ahl, b32, outgoing, arrived, term, far_l, far_r, far_l2, far_r2, near_l, near_r, crossed, from_y, held,
    local, slot2, slot3, slot4, acc2, acc3, part,
    round_sem, a_sem, b_sem, small_sem, out_sem, keep_sem, ex_send, ex_recv, far_send, far_recv, near_send, near_recv,
    cross_send, cross_recv, y_send, y_recv, send2, recv2, send3, recv3, send4, recv4, send5, recv5,
):
    pole = lax.axis_index("pole")
    sub = lax.axis_index("sub")
    x = pole // 2
    yl = pole % 2
    other = 1 - yl
    yh = sub // 16
    z = (sub // 2) % 8
    core = sub % 2
    y = yh * 2 + yl
    here = x * 2 + core
    nxt = (sub + 1) % NSUB
    prv = (sub + NSUB - 1) % NSUB
    right = ((x + 1) % NX) * 2 + yl
    left = ((x + NX - 1) % NX) * 2 + yl
    across = x * 2 + other

    def at_xc(d):
        t = (here + d) % 8
        return t, ((t // 2) * 2 + yl, (yh * 8 + z) * 2 + t % 2)

    def at_y(d):
        t = (y + d) % 4
        return (x * 2 + t % 2, ((t // 2) * 8 + z) * 2 + core)

    def at_z(d):
        t = (z + d) % 8
        return (pole, (yh * 8 + t) * 2 + core)

    def fetch(s):
        return (
            pltpu.make_async_copy(inv_ref.at[s], a32.at[s], a_sem.at[s]),
            pltpu.make_async_copy(start_ref.at[s], b32.at[s], b_sem.at[s]),
        )

    small = [
        pltpu.make_async_copy(src, dst, small_sem.at[i])
        for i, (src, dst) in enumerate(
            ((rows_hbm, rows_ref), (coup_hbm, coup_ref), (nb_hbm, nb_ref), (w_hbm, w_ref))
        )
    ]
    for copy in fetch(0):
        copy.start()
    for copy in small:
        copy.start()
    barrier = pltpu.get_barrier_semaphore()
    z_near = (at_z(1), at_z(7))
    peers = [(pole, nxt), (pole, prv), *z_near, at_y(1), at_y(3), (right, sub), (left, sub)]
    for dev in peers:
        pl.semaphore_signal(barrier, inc=1, device_id=dev, device_id_type=MESH)
    for s in range(1, SUB):
        for copy in fetch(s):
            copy.start()

    def tell(n):
        for dev in z_near:
            pl.semaphore_signal(round_sem.at[n], inc=1, device_id=dev, device_id_type=MESH)

    def hear(n):
        pl.semaphore_wait(round_sem.at[n], 2)

    def send(src, dst, s_sem, r_sem, dev):
        return pltpu.make_async_remote_copy(
            src_ref=src, dst_ref=dst, send_sem=s_sem, recv_sem=r_sem,
            device_id=dev, device_id_type=MESH,
        )

    def exchange(side, s):
        return send(
            outgoing.at[side, s], arrived.at[1 - side, s],
            ex_send.at[side, s], ex_recv.at[1 - side, s],
            (pole, prv if side == 0 else nxt),
        )

    lane_ids = lax.broadcasted_iota(jnp.int32, (IFC, BLK), 1).astype(F32)
    row_ids = lax.broadcasted_iota(jnp.int32, (BLK, 2 * IFC), 0)

    def apply(s, vectors):
        parts = pair(vectors)
        return fold(mm(ahl[s, :, :BLK], parts)) + mm(ahl[s, :, BLK:], parts[:, :VEC])

    def first(s, carry):
        for copy in fetch(s):
            copy.wait()
        a = a32[s]
        high = a.astype(BF16)
        ahl[s, :, :BLK] = high
        ahl[s, :, BLK:] = (a - high.astype(F32)).astype(BF16)
        parts = pair(apply(s, b32[s]))
        rows = rows_ref[s].astype(F32)
        for side in range(2):
            ids = down_lanes(rows[side : side + 1])
            pick = (lane_ids == jnp.concatenate([ids] * (BLK // IFC), axis=1)).astype(F32).astype(BF16)
            outgoing[side, s] = fold(mm(pick, parts))

        @pl.when(s == 0)
        def _():
            pl.semaphore_wait(barrier, len(peers))
            tell(0)

        for side in range(2):
            exchange(side, s).start()
        return carry

    for copy in small:
        copy.wait()
    lax.fori_loop(0, SUB, first, 0)
    hear(0)
    tell(1)

    def arrive(s, carry):
        exchange(0, s).wait()
        exchange(1, s).wait()
        return carry

    lax.fori_loop(0, SUB, arrive, 0)

    weight = w_ref[0]

    def second(s):
        rows = rows_ref[s]
        coup = coup_ref[s]
        low = arrived[0, lax.rem(nb_ref[0, s], SUB)] * down_lanes(coup[0:1])
        high = arrived[1, lax.rem(nb_ref[1, s], SUB)] * down_lanes(coup[1:2])
        terms = pair(jnp.concatenate([low, high], axis=0))
        row = jnp.concatenate([rows[0:1], rows[1:2]], axis=1)
        place = (row_ids == row).astype(F32).astype(BF16)
        term[s] = weight * apply(s, b32[s] + fold(mm(place, terms)))

    def owner(shift, kind):
        return ((x + shift) % NX) * 2 + (other if kind == 0 else yl)

    lo, hi = pl.ds(0, XROWS // 2), pl.ds(XROWS // 2, XROWS // 2)
    ylo, yhi = pl.ds(XROWS, YROWS // 2), pl.ds(XROWS + YROWS // 2, YROWS // 2)
    xrows, yrows = pl.ds(0, XROWS), pl.ds(XROWS, YROWS)

    def far(kind):
        s = owner(2, min(kind, 1))
        to_r, to_l = (lo, hi) if kind < 2 else (ylo, yhi)
        dst_r = far_l.at[kind] if kind < 2 else far_l2
        dst_l = far_r.at[kind] if kind < 2 else far_r2
        return (
            send(term.at[s, to_r], dst_r, far_send.at[0, kind], far_recv.at[0, kind], (right, sub)),
            send(term.at[s, to_l], dst_l, far_send.at[1, kind], far_recv.at[1, kind], (left, sub)),
        )

    def near(kind, step):
        low, high = (lo, hi) if kind < 2 else (ylo, yhi)
        to_r, to_l = (high, low) if step == 0 else (low, high)
        s, slot = min(kind, 1), min(kind, 1)
        return (
            send(term.at[owner(1, s), to_r], near_l.at[slot, to_r], near_send.at[0, kind, step],
                 near_recv.at[0, kind, step], (right, sub)),
            send(term.at[owner(3, s), to_l], near_r.at[slot, to_l], near_send.at[1, kind, step],
                 near_recv.at[1, kind, step], (left, sub)),
        )

    def cross(shift):
        return send(
            term.at[owner(shift, 0), yrows], crossed.at[shift],
            cross_send.at[shift], cross_recv.at[shift], (across, sub),
        )

    def relay(kind):
        far_a, far_b = far(kind)
        low, high = (lo, hi) if kind < 2 else (ylo, yhi)
        s = owner(1, min(kind, 1))
        far_a.wait_recv()
        term[s, low] = term[s, low] + (far_l[kind] if kind < 2 else far_l2[...])
        near(kind, 1)[0].start()
        s = owner(3, min(kind, 1))
        far_b.wait_recv()
        term[s, high] = term[s, high] + (far_r[kind] if kind < 2 else far_r2[...])
        near(kind, 1)[1].start()

    def join(shift):
        cross(shift).wait_recv()
        s = owner(shift, 1)
        term[s, yrows] = term[s, yrows] + crossed[shift]

    def sequence(i, carry):
        shift = jnp.where(i < 2, 2, jnp.where(i < 5, (2 * i - 3) % 4, (2 * i - 9) % 4))
        shift = jnp.where((i == 4) | (i == 7), 0, shift)
        kind = jnp.where((i == 1) | (i > 4), 1, 0)

        @pl.when(i == 7)
        def _():
            relay(0)

        second(((x + shift) % NX) * 2 + jnp.where(kind == 0, other, yl))

        @pl.when(i == 0)
        def _():
            far(0)[0].start()
            far(0)[1].start()
            cross(2).start()

        @pl.when(i == 1)
        def _():
            far(1)[0].start()
            far(1)[1].start()

        @pl.when(i == 2)
        def _():
            near(0, 0)[0].start()
            cross(1).start()

        @pl.when(i == 3)
        def _():
            near(0, 0)[1].start()
            cross(3).start()

        @pl.when(i == 4)
        def _():
            cross(0).start()
        return carry

    lax.fori_loop(0, SUB, sequence, 0)
    hear(1)
    tell(2)

    join(2)
    for copy in far(2) + near(1, 0):
        copy.start()
    relay(1)
    join(1)
    near(2, 0)[0].start()
    join(3)
    near(2, 0)[1].start()

    own = owner(0, 0)
    for copy in near(0, 0) + near(0, 1):
        copy.wait_recv()
    term[own, xrows] = term[own, xrows] + near_l[0, xrows] + near_r[0, xrows]
    hand = send(term.at[own, xrows], from_y, y_send, y_recv, (across, sub))
    hand.start()
    relay(2)
    join(0)
    for copy in near(1, 0) + near(1, 1) + near(2, 0) + near(2, 1):
        copy.wait_recv()
    own = owner(0, 1)
    hand.wait_recv()
    term[own, xrows] = term[own, xrows] + from_y[...]
    mine = term[own] + near_l[1] + near_r[1]
    held[...] = mine
    leave = pltpu.make_async_copy(held, out_ref, out_sem)
    leave.start()
    hear(2)

    parts = pair(mine)
    four = lax.dot_general(parts, parts, (((0,), (0,)), ((), ())), preferred_element_type=F32)
    local[...] = fold(four[:VEC]) + fold(four[VEC:])

    def rows_of(n):
        return pl.ds(pl.multiple_of(n * PIECE, PIECE), PIECE)

    copies2 = []
    for d in range(1, 8):
        t, dev = at_xc(d)
        copies2.append(send(local.at[rows_of(t)], slot2.at[d - 1], send2.at[d - 1], recv2.at[d - 1], dev))
    for d in EIGHT:
        copies2[d - 1].start()
    total = local[rows_of(here)]
    for d in range(7):
        copies2[d].wait_recv()
        total = total + slot2[d]
    acc2[...] = total

    copies3 = [
        send(acc2, slot3.at[d - 1], send3.at[d - 1], recv3.at[d - 1], at_y(d)) for d in range(1, 4)
    ]
    for d in FOUR:
        copies3[d - 1].start()
    for d in range(3):
        copies3[d].wait_recv()
        total = total + slot3[d]
    acc3[...] = total

    copies4 = [
        send(acc3, slot4.at[d - 1], send4.at[d - 1], recv4.at[d - 1], at_z(d)) for d in range(1, 8)
    ]
    for d in EIGHT:
        copies4[d - 1].start()
    for d in range(7):
        copies4[d].wait_recv()
        total = total + slot4[d]
    part[...] = total
    keep = pltpu.make_async_copy(part, gram_ref.at[rows_of(here)], keep_sem)
    keep.start()

    copies5 = [
        send(part, gram_ref.at[rows_of(here)], send5.at[d - 1], recv5.at[d - 1], at_xc(d)[1])
        for d in range(1, 8)
    ]
    for d in EIGHT:
        copies5[d - 1].start()
    hand.wait_send()
    for kind in range(3):
        for copy in far(kind) + near(kind, 0) + near(kind, 1):
            copy.wait_send()
    for shift in range(NX):
        cross(shift).wait_send()
    for copy in copies2 + copies3 + copies4:
        copy.wait_send()
    leave.wait()
    keep.wait()
    for copy in copies5:
        copy.wait()


def filter_call(neighbors, pole_weights, iface_rows, couplings, start, inverses):
    dma = pltpu.SemaphoreType.DMA
    hbm = pl.BlockSpec(memory_space=pltpu.HBM)
    return pl.pallas_call(
        filter_kernel,
        name="filter_pass",
        out_shape=(
            jax.ShapeDtypeStruct((BLK, VEC), F32),
            jax.ShapeDtypeStruct((VEC, VEC), F32),
        ),
        in_specs=[hbm] * 6,
        out_specs=(hbm, hbm),
        scratch_shapes=[
            pltpu.SMEM((2, SUB), jnp.int32),
            pltpu.SMEM((1,), F32),
            pltpu.VMEM((SUB, 2, IFC), jnp.int32),
            pltpu.VMEM((SUB, 2, IFC), F32),
            pltpu.VMEM((SUB, BLK, BLK), F32),
            pltpu.VMEM((SUB, BLK, 2 * BLK), BF16),
            pltpu.VMEM((SUB, BLK, VEC), F32),
            pltpu.VMEM((2, SUB, IFC, VEC), F32),
            pltpu.VMEM((2, SUB, IFC, VEC), F32),
            pltpu.VMEM((SUB, BLK, VEC), F32),
            pltpu.VMEM((2, XROWS // 2, VEC), F32),
            pltpu.VMEM((2, XROWS // 2, VEC), F32),
            pltpu.VMEM((YROWS // 2, VEC), F32),
            pltpu.VMEM((YROWS // 2, VEC), F32),
            pltpu.VMEM((2, BLK, VEC), F32),
            pltpu.VMEM((2, BLK, VEC), F32),
            pltpu.VMEM((NX, YROWS, VEC), F32),
            pltpu.VMEM((XROWS, VEC), F32),
            pltpu.VMEM((BLK, VEC), F32),
            pltpu.VMEM((VEC, VEC), F32),
            pltpu.VMEM((7, PIECE, VEC), F32),
            pltpu.VMEM((3, PIECE, VEC), F32),
            pltpu.VMEM((7, PIECE, VEC), F32),
            pltpu.VMEM((PIECE, VEC), F32),
            pltpu.VMEM((PIECE, VEC), F32),
            pltpu.VMEM((PIECE, VEC), F32),
            pltpu.SemaphoreType.REGULAR((3,)),
            dma((SUB,)), dma((SUB,)), dma((4,)), dma, dma,
            dma((2, SUB)), dma((2, SUB)),
            dma((2, 3)), dma((2, 3)),
            dma((2, 3, 2)), dma((2, 3, 2)),
            dma((NX,)), dma((NX,)), dma, dma,
            dma((7,)), dma((7,)), dma((3,)), dma((3,)),
            dma((7,)), dma((7,)), dma((7,)), dma((7,)),
        ],
        compiler_params=pltpu.CompilerParams(
            collective_id=0, has_side_effects=True, vmem_limit_bytes=56 * 1024 * 1024
        ),
    )(neighbors, pole_weights, iface_rows, couplings, start, inverses)


TILE = 8
PANEL = 16
CLOSE = 2


def spread(row):
    return jnp.broadcast_to(row, (TILE, VEC))


def three(value):
    first = value.astype(BF16)
    rest = value - first.astype(F32)
    second = rest.astype(BF16)
    return first, second, (rest - second.astype(F32)).astype(BF16)


def six_terms(a, b, axis):
    a1, a2, a3 = three(a)
    b1, b2, b3 = three(b)
    return (
        jnp.concatenate([a1, a1, a2, a1, a3, a2], axis=axis),
        jnp.concatenate([b1, b2, b1, b3, b1, b2], axis=axis),
    )


def ortho_kernel(scale, g_ref, f_ref, out_ref, w_ref):
    count, tall = VEC // TILE, PANEL // TILE
    tiles = [g_ref[TILE * t : TILE * t + TILE, :] for t in range(count)]
    sub = lax.broadcasted_iota(jnp.int32, (TILE, VEC), 0)
    lane = lax.broadcasted_iota(jnp.int32, (TILE, VEC), 1)
    below = [(sub > k).astype(F32) for k in range(TILE)]
    for p in range(0, count, tall):
        c0 = TILE * p
        own = list(range(p, p + tall))
        close = list(range(p + tall, min(count, p + tall + CLOSE)))
        cols = {
            (m, t): jnp.broadcast_to(tiles[t][:, c0 + m : c0 + m + 1], (TILE, VEC))
            for t in own + close
            for m in range(PANEL)
        }
        panel = (lane >= c0) & (lane < c0 + PANEL)
        top = {t: jnp.where(panel, (lane == sub + TILE * t).astype(F32), tiles[t]) for t in own}
        pivots = {t: jnp.ones((TILE, VEC), F32) for t in own}
        inverses = dict(pivots)
        factors, rows = {}, []
        for k in range(PANEL):
            t0, r = p + k // TILE, k % TILE
            pivot = spread(cols[k, t0][r : r + 1])
            inverse = 1.0 / pivot
            pivots[t0] = jnp.where(sub == r, pivot, pivots[t0])
            inverses[t0] = jnp.where(sub == r, inverse, inverses[t0])
            upper = {m: spread(cols[m, t0][r : r + 1]) for m in range(k + 1, PANEL)}
            row = spread(top[t0][r : r + 1])
            rows.append(row)
            for t in range(t0, p + tall):
                for m in range(k + 1, PANEL):
                    cols[m, t] = cols[m, t] - (cols[k, t] * upper[m]) * inverse
                column = cols[k, t] * below[r] if t == t0 else cols[k, t]
                top[t] = top[t] - (column * row) * inverse
            for t in close:
                f = cols[k, t] * inverse
                factors[k, t] = f
                for m in range(k + 1, PANEL):
                    cols[m, t] = cols[m, t] - f * upper[m]
        for t in close:
            terms = [factors[k, t] * rows[k] for k in range(PANEL)]
            while len(terms) > 1:
                terms = [terms[i] + terms[i + 1] for i in range(0, len(terms), 2)]
            tiles[t] = jnp.where(panel, 0.0, tiles[t]) - terms[0]
        distant = p + tall + CLOSE
        if distant < count:
            final = jnp.concatenate([top[t] for t in own], axis=0)
            a, b = six_terms(final * jnp.concatenate([inverses[t] for t in own], axis=0), final, 0)
            update = lax.dot_general(a, b, (((0,), (0,)), ((), ())), preferred_element_type=F32)
            for t in range(distant, count):
                tiles[t] = jnp.where(panel, 0.0, tiles[t]) - update[TILE * t : TILE * t + TILE]
        for t in own:
            w_ref[TILE * t : TILE * t + TILE, :] = jnp.where(
                lane <= sub + TILE * t, top[t] * (scale * lax.rsqrt(pivots[t])), 0.0
            )
    a1, a2, a3 = three(f_ref[...])
    b1, b2, b3 = three(w_ref[...])
    along = (((1,), (1,)), ((), ()))
    wide = lax.dot_general(
        jnp.concatenate([a1, a2], axis=1),
        jnp.concatenate([jnp.concatenate([b1, b1], axis=1), jnp.concatenate([b2, b2], axis=1)], axis=0),
        along, preferred_element_type=F32,
    )
    small = lax.dot_general(
        jnp.concatenate([a1, a3], axis=1), jnp.concatenate([b3, b1], axis=1),
        along, preferred_element_type=F32,
    )
    out_ref[...] = wide[:, :VEC] + (wide[:, VEC:] + small)


def ortho_call(gram_matrix, filtered, scale):
    vmem = pl.BlockSpec(memory_space=pltpu.VMEM)
    return pl.pallas_call(
        functools.partial(ortho_kernel, scale),
        name="ortho",
        out_shape=jax.ShapeDtypeStruct((BLK, VEC), F32),
        in_specs=[vmem, vmem],
        out_specs=vmem,
        scratch_shapes=[pltpu.VMEM((VEC, VEC), F32)],
    )(gram_matrix, filtered)


def per_device(start_block, inverses, iface_rows, neighbors, couplings, pole_weights):
    filtered, gram_matrix = filter_call(
        neighbors.T, pole_weights, iface_rows, couplings,
        start_block.reshape(SUB, BLK, VEC), inverses[0],
    )
    return ortho_call(gram_matrix, filtered, math.sqrt(NSUB * SUB * BLK))


def solution(mesh):
    placed = (
        P("sub", None),
        P("pole", "sub", None, None),
        P("sub", None, None),
        P("sub", None),
        P("sub", None, None),
        P("pole"),
    )
    return jax.shard_map(
        per_device, mesh=mesh, in_specs=placed, out_specs=P(("sub", "pole"), None), check_vma=False
    )
```

```python
import functools
import math

import jax
import jax.numpy as jnp
from jax import lax
from jax.experimental import pallas as pl
from jax.experimental.pallas import tpu as pltpu
from jax.sharding import PartitionSpec as P

precise = lax.Precision.HIGHEST
MESH = pl.DeviceIdType.MESH
F32 = jnp.float32
BF16 = jnp.bfloat16

SUB = 8
BLK = 512
VEC = 128
IFC = 128
PIECE = VEC // 8
EIGHT = (4, 3, 5, 2, 6, 1, 7)
FOUR = (2, 1, 3)
XROWS = 288
YROWS = BLK - XROWS
NX = 4
NSUB = 32


def pair(value):
    high = value.astype(BF16)
    low = (value - high.astype(F32)).astype(BF16)
    return jnp.concatenate([high, low], axis=1)


def fold(wide):
    return wide[:, :VEC] + wide[:, VEC:]


def mm(a, b):
    return jnp.dot(a, b, preferred_element_type=F32)


def down_lanes(row):
    return jnp.broadcast_to(row, (IFC, IFC)).T


def filter_kernel(
    nb_hbm, w_hbm, rows_hbm, coup_hbm, start_ref, inv_ref, out_ref, gram_ref,
    nb_ref, w_ref, rows_ref, coup_ref, a32, ahl, b32, outgoing, arrived, term, far_l, far_r, far_l2, far_r2, near_l, near_r, crossed, from_y, held,
    local, slot2, slot3, slot4, acc2, acc3, part,
    round_sem, a_sem, b_sem, small_sem, out_sem, keep_sem, ex_send, ex_recv, far_send, far_recv, near_send, near_recv,
    cross_send, cross_recv, y_send, y_recv, send2, recv2, send3, recv3, send4, recv4, send5, recv5,
):
    pole = lax.axis_index("pole")
    sub = lax.axis_index("sub")
    x = pole // 2
    yl = pole % 2
    other = 1 - yl
    yh = sub // 16
    z = (sub // 2) % 8
    core = sub % 2
    y = yh * 2 + yl
    here = x * 2 + core
    nxt = (sub + 1) % NSUB
    prv = (sub + NSUB - 1) % NSUB
    right = ((x + 1) % NX) * 2 + yl
    left = ((x + NX - 1) % NX) * 2 + yl
    across = x * 2 + other

    def at_xc(d):
        t = (here + d) % 8
        return t, ((t // 2) * 2 + yl, (yh * 8 + z) * 2 + t % 2)

    def at_y(d):
        t = (y + d) % 4
        return (x * 2 + t % 2, ((t // 2) * 8 + z) * 2 + core)

    def at_z(d):
        t = (z + d) % 8
        return (pole, (yh * 8 + t) * 2 + core)

    def fetch(s):
        return (
            pltpu.make_async_copy(inv_ref.at[s], a32.at[s], a_sem.at[s]),
            pltpu.make_async_copy(start_ref.at[s], b32.at[s], b_sem.at[s]),
        )

    small = [
        pltpu.make_async_copy(src, dst, small_sem.at[i])
        for i, (src, dst) in enumerate(
            ((rows_hbm, rows_ref), (coup_hbm, coup_ref), (nb_hbm, nb_ref), (w_hbm, w_ref))
        )
    ]
    for copy in fetch(0):
        copy.start()
    for copy in small:
        copy.start()
    barrier = pltpu.get_barrier_semaphore()
    z_near = (at_z(1), at_z(7))
    peers = [(pole, nxt), (pole, prv), *z_near, at_y(1), at_y(3), (right, sub), (left, sub)]
    for dev in peers:
        pl.semaphore_signal(barrier, inc=1, device_id=dev, device_id_type=MESH)
    for s in range(1, SUB):
        for copy in fetch(s):
            copy.start()

    def tell(n):
        for dev in z_near:
            pl.semaphore_signal(round_sem.at[n], inc=1, device_id=dev, device_id_type=MESH)

    def hear(n):
        pl.semaphore_wait(round_sem.at[n], 2)

    def send(src, dst, s_sem, r_sem, dev):
        return pltpu.make_async_remote_copy(
            src_ref=src, dst_ref=dst, send_sem=s_sem, recv_sem=r_sem,
            device_id=dev, device_id_type=MESH,
        )

    def exchange(side, s):
        return send(
            outgoing.at[side, s], arrived.at[1 - side, s],
            ex_send.at[side, s], ex_recv.at[1 - side, s],
            (pole, prv if side == 0 else nxt),
        )

    lane_ids = lax.broadcasted_iota(jnp.int32, (IFC, BLK), 1).astype(F32)
    row_ids = lax.broadcasted_iota(jnp.int32, (BLK, 2 * IFC), 0)

    def apply(s, vectors):
        parts = pair(vectors)
        return fold(mm(ahl[s, :, :BLK], parts)) + mm(ahl[s, :, BLK:], parts[:, :VEC])

    def first(s, carry):
        for copy in fetch(s):
            copy.wait()
        a = a32[s]
        high = a.astype(BF16)
        ahl[s, :, :BLK] = high
        ahl[s, :, BLK:] = (a - high.astype(F32)).astype(BF16)
        parts = pair(apply(s, b32[s]))
        rows = rows_ref[s].astype(F32)
        for side in range(2):
            ids = down_lanes(rows[side : side + 1])
            pick = (lane_ids == jnp.concatenate([ids] * (BLK // IFC), axis=1)).astype(F32).astype(BF16)
            outgoing[side, s] = fold(mm(pick, parts))

        @pl.when(s == 0)
        def _():
            pl.semaphore_wait(barrier, len(peers))
            tell(0)

        for side in range(2):
            exchange(side, s).start()
        return carry

    for copy in small:
        copy.wait()
    lax.fori_loop(0, SUB, first, 0)
    hear(0)
    tell(1)

    def arrive(s, carry):
        exchange(0, s).wait()
        exchange(1, s).wait()
        return carry

    lax.fori_loop(0, SUB, arrive, 0)

    weight = w_ref[0]

    def second(s):
        rows = rows_ref[s]
        coup = coup_ref[s]
        low = arrived[0, lax.rem(nb_ref[0, s], SUB)] * down_lanes(coup[0:1])
        high = arrived[1, lax.rem(nb_ref[1, s], SUB)] * down_lanes(coup[1:2])
        terms = pair(jnp.concatenate([low, high], axis=0))
        row = jnp.concatenate([rows[0:1], rows[1:2]], axis=1)
        place = (row_ids == row).astype(F32).astype(BF16)
        term[s] = weight * apply(s, b32[s] + fold(mm(place, terms)))

    def owner(shift, kind):
        return ((x + shift) % NX) * 2 + (other if kind == 0 else yl)

    lo, hi = pl.ds(0, XROWS // 2), pl.ds(XROWS // 2, XROWS // 2)
    ylo, yhi = pl.ds(XROWS, YROWS // 2), pl.ds(XROWS + YROWS // 2, YROWS // 2)
    xrows, yrows = pl.ds(0, XROWS), pl.ds(XROWS, YROWS)

    def far(kind):
        s = owner(2, min(kind, 1))
        to_r, to_l = (lo, hi) if kind < 2 else (ylo, yhi)
        dst_r = far_l.at[kind] if kind < 2 else far_l2
        dst_l = far_r.at[kind] if kind < 2 else far_r2
        return (
            send(term.at[s, to_r], dst_r, far_send.at[0, kind], far_recv.at[0, kind], (right, sub)),
            send(term.at[s, to_l], dst_l, far_send.at[1, kind], far_recv.at[1, kind], (left, sub)),
        )

    def near(kind, step):
        low, high = (lo, hi) if kind < 2 else (ylo, yhi)
        to_r, to_l = (high, low) if step == 0 else (low, high)
        s, slot = min(kind, 1), min(kind, 1)
        return (
            send(term.at[owner(1, s), to_r], near_l.at[slot, to_r], near_send.at[0, kind, step],
                 near_recv.at[0, kind, step], (right, sub)),
            send(term.at[owner(3, s), to_l], near_r.at[slot, to_l], near_send.at[1, kind, step],
                 near_recv.at[1, kind, step], (left, sub)),
        )

    def cross(shift):
        return send(
            term.at[owner(shift, 0), yrows], crossed.at[shift],
            cross_send.at[shift], cross_recv.at[shift], (across, sub),
        )

    def relay(kind):
        far_a, far_b = far(kind)
        low, high = (lo, hi) if kind < 2 else (ylo, yhi)
        s = owner(1, min(kind, 1))
        far_a.wait_recv()
        term[s, low] = term[s, low] + (far_l[kind] if kind < 2 else far_l2[...])
        near(kind, 1)[0].start()
        s = owner(3, min(kind, 1))
        far_b.wait_recv()
        term[s, high] = term[s, high] + (far_r[kind] if kind < 2 else far_r2[...])
        near(kind, 1)[1].start()

    def join(shift):
        cross(shift).wait_recv()
        s = owner(shift, 1)
        term[s, yrows] = term[s, yrows] + crossed[shift]

    def sequence(i, carry):
        shift = jnp.where(i < 2, 2, jnp.where(i < 5, (2 * i - 3) % 4, (2 * i - 9) % 4))
        shift = jnp.where((i == 4) | (i == 7), 0, shift)
        kind = jnp.where((i == 1) | (i > 4), 1, 0)

        @pl.when(i == 6)
        def _():
            relay(0)

        second(((x + shift) % NX) * 2 + jnp.where(kind == 0, other, yl))

        @pl.when(i == 0)
        def _():
            far(0)[0].start()
            far(0)[1].start()
            cross(2).start()

        @pl.when(i == 1)
        def _():
            far(1)[0].start()
            far(1)[1].start()

        @pl.when(i == 2)
        def _():
            near(0, 0)[0].start()
            cross(1).start()

        @pl.when(i == 3)
        def _():
            near(0, 0)[1].start()
            cross(3).start()

        @pl.when(i == 4)
        def _():
            cross(0).start()
        return carry

    lax.fori_loop(0, SUB, sequence, 0)
    hear(1)
    tell(2)

    join(2)
    for copy in far(2) + near(1, 0):
        copy.start()
    relay(1)
    join(1)
    near(2, 0)[0].start()
    join(3)
    near(2, 0)[1].start()

    own = owner(0, 0)
    for copy in near(0, 0) + near(0, 1):
        copy.wait_recv()
    term[own, xrows] = term[own, xrows] + near_l[0, xrows] + near_r[0, xrows]
    hand = send(term.at[own, xrows], from_y, y_send, y_recv, (across, sub))
    hand.start()
    relay(2)
    join(0)
    for copy in near(1, 0) + near(1, 1) + near(2, 0) + near(2, 1):
        copy.wait_recv()
    own = owner(0, 1)
    hand.wait_recv()
    term[own, xrows] = term[own, xrows] + from_y[...]
    mine = term[own] + near_l[1] + near_r[1]
    held[...] = mine
    leave = pltpu.make_async_copy(held, out_ref, out_sem)
    leave.start()
    hear(2)

    parts = pair(mine)
    four = lax.dot_general(parts, parts, (((0,), (0,)), ((), ())), preferred_element_type=F32)
    local[...] = fold(four[:VEC]) + fold(four[VEC:])

    def rows_of(n):
        return pl.ds(pl.multiple_of(n * PIECE, PIECE), PIECE)

    copies2 = []
    for d in range(1, 8):
        t, dev = at_xc(d)
        copies2.append(send(local.at[rows_of(t)], slot2.at[d - 1], send2.at[d - 1], recv2.at[d - 1], dev))
    for d in EIGHT:
        copies2[d - 1].start()
    total = local[rows_of(here)]
    for d in range(7):
        copies2[d].wait_recv()
        total = total + slot2[d]
    acc2[...] = total

    copies3 = [
        send(acc2, slot3.at[d - 1], send3.at[d - 1], recv3.at[d - 1], at_y(d)) for d in range(1, 4)
    ]
    for d in FOUR:
        copies3[d - 1].start()
    for d in range(3):
        copies3[d].wait_recv()
        total = total + slot3[d]
    acc3[...] = total

    copies4 = [
        send(acc3, slot4.at[d - 1], send4.at[d - 1], recv4.at[d - 1], at_z(d)) for d in range(1, 8)
    ]
    for d in EIGHT:
        copies4[d - 1].start()
    for d in range(7):
        copies4[d].wait_recv()
        total = total + slot4[d]
    part[...] = total
    keep = pltpu.make_async_copy(part, gram_ref.at[rows_of(here)], keep_sem)
    keep.start()

    copies5 = [
        send(part, gram_ref.at[rows_of(here)], send5.at[d - 1], recv5.at[d - 1], at_xc(d)[1])
        for d in range(1, 8)
    ]
    for d in EIGHT:
        copies5[d - 1].start()
    hand.wait_send()
    for kind in range(3):
        for copy in far(kind) + near(kind, 0) + near(kind, 1):
            copy.wait_send()
    for shift in range(NX):
        cross(shift).wait_send()
    for copy in copies2 + copies3 + copies4:
        copy.wait_send()
    leave.wait()
    keep.wait()
    for copy in copies5:
        copy.wait()


def filter_call(neighbors, pole_weights, iface_rows, couplings, start, inverses):
    dma = pltpu.SemaphoreType.DMA
    hbm = pl.BlockSpec(memory_space=pltpu.HBM)
    return pl.pallas_call(
        filter_kernel,
        name="filter_pass",
        out_shape=(
            jax.ShapeDtypeStruct((BLK, VEC), F32),
            jax.ShapeDtypeStruct((VEC, VEC), F32),
        ),
        in_specs=[hbm] * 6,
        out_specs=(hbm, hbm),
        scratch_shapes=[
            pltpu.SMEM((2, SUB), jnp.int32),
            pltpu.SMEM((1,), F32),
            pltpu.VMEM((SUB, 2, IFC), jnp.int32),
            pltpu.VMEM((SUB, 2, IFC), F32),
            pltpu.VMEM((SUB, BLK, BLK), F32),
            pltpu.VMEM((SUB, BLK, 2 * BLK), BF16),
            pltpu.VMEM((SUB, BLK, VEC), F32),
            pltpu.VMEM((2, SUB, IFC, VEC), F32),
            pltpu.VMEM((2, SUB, IFC, VEC), F32),
            pltpu.VMEM((SUB, BLK, VEC), F32),
            pltpu.VMEM((2, XROWS // 2, VEC), F32),
            pltpu.VMEM((2, XROWS // 2, VEC), F32),
            pltpu.VMEM((YROWS // 2, VEC), F32),
            pltpu.VMEM((YROWS // 2, VEC), F32),
            pltpu.VMEM((2, BLK, VEC), F32),
            pltpu.VMEM((2, BLK, VEC), F32),
            pltpu.VMEM((NX, YROWS, VEC), F32),
            pltpu.VMEM((XROWS, VEC), F32),
            pltpu.VMEM((BLK, VEC), F32),
            pltpu.VMEM((VEC, VEC), F32),
            pltpu.VMEM((7, PIECE, VEC), F32),
            pltpu.VMEM((3, PIECE, VEC), F32),
            pltpu.VMEM((7, PIECE, VEC), F32),
            pltpu.VMEM((PIECE, VEC), F32),
            pltpu.VMEM((PIECE, VEC), F32),
            pltpu.VMEM((PIECE, VEC), F32),
            pltpu.SemaphoreType.REGULAR((3,)),
            dma((SUB,)), dma((SUB,)), dma((4,)), dma, dma,
            dma((2, SUB)), dma((2, SUB)),
            dma((2, 3)), dma((2, 3)),
            dma((2, 3, 2)), dma((2, 3, 2)),
            dma((NX,)), dma((NX,)), dma, dma,
            dma((7,)), dma((7,)), dma((3,)), dma((3,)),
            dma((7,)), dma((7,)), dma((7,)), dma((7,)),
        ],
        compiler_params=pltpu.CompilerParams(
            collective_id=0, has_side_effects=True, vmem_limit_bytes=56 * 1024 * 1024
        ),
    )(neighbors, pole_weights, iface_rows, couplings, start, inverses)


TILE = 8
PANEL = 16
CLOSE = 2


def spread(row):
    return jnp.broadcast_to(row, (TILE, VEC))


def three(value):
    first = value.astype(BF16)
    rest = value - first.astype(F32)
    second = rest.astype(BF16)
    return first, second, (rest - second.astype(F32)).astype(BF16)


def six_terms(a, b, axis):
    a1, a2, a3 = three(a)
    b1, b2, b3 = three(b)
    return (
        jnp.concatenate([a1, a1, a2, a1, a3, a2], axis=axis),
        jnp.concatenate([b1, b2, b1, b3, b1, b2], axis=axis),
    )


def ortho_kernel(scale, g_ref, f_ref, out_ref, w_ref):
    count, tall = VEC // TILE, PANEL // TILE
    tiles = [g_ref[TILE * t : TILE * t + TILE, :] for t in range(count)]
    sub = lax.broadcasted_iota(jnp.int32, (TILE, VEC), 0)
    lane = lax.broadcasted_iota(jnp.int32, (TILE, VEC), 1)
    below = [(sub > k).astype(F32) for k in range(TILE)]
    for p in range(0, count, tall):
        c0 = TILE * p
        own = list(range(p, p + tall))
        close = list(range(p + tall, min(count, p + tall + CLOSE)))
        cols = {
            (m, t): jnp.broadcast_to(tiles[t][:, c0 + m : c0 + m + 1], (TILE, VEC))
            for t in own + close
            for m in range(PANEL)
        }
        panel = (lane >= c0) & (lane < c0 + PANEL)
        top = {t: jnp.where(panel, (lane == sub + TILE * t).astype(F32), tiles[t]) for t in own}
        pivots = {t: jnp.ones((TILE, VEC), F32) for t in own}
        inverses = dict(pivots)
        factors, rows = {}, []
        for k in range(PANEL):
            t0, r = p + k // TILE, k % TILE
            pivot = spread(cols[k, t0][r : r + 1])
            inverse = 1.0 / pivot
            pivots[t0] = jnp.where(sub == r, pivot, pivots[t0])
            inverses[t0] = jnp.where(sub == r, inverse, inverses[t0])
            upper = {m: spread(cols[m, t0][r : r + 1]) for m in range(k + 1, PANEL)}
            row = spread(top[t0][r : r + 1])
            rows.append(row)
            for t in range(t0, p + tall):
                for m in range(k + 1, PANEL):
                    cols[m, t] = cols[m, t] - (cols[k, t] * upper[m]) * inverse
                column = cols[k, t] * below[r] if t == t0 else cols[k, t]
                top[t] = top[t] - (column * row) * inverse
            for t in close:
                f = cols[k, t] * inverse
                factors[k, t] = f
                for m in range(k + 1, PANEL):
                    cols[m, t] = cols[m, t] - f * upper[m]
        for t in close:
            terms = [factors[k, t] * rows[k] for k in range(PANEL)]
            while len(terms) > 1:
                terms = [terms[i] + terms[i + 1] for i in range(0, len(terms), 2)]
            tiles[t] = jnp.where(panel, 0.0, tiles[t]) - terms[0]
        distant = p + tall + CLOSE
        if distant < count:
            final = jnp.concatenate([top[t] for t in own], axis=0)
            a, b = six_terms(final * jnp.concatenate([inverses[t] for t in own], axis=0), final, 0)
            update = lax.dot_general(a, b, (((0,), (0,)), ((), ())), preferred_element_type=F32)
            for t in range(distant, count):
                tiles[t] = jnp.where(panel, 0.0, tiles[t]) - update[TILE * t : TILE * t + TILE]
        for t in own:
            w_ref[TILE * t : TILE * t + TILE, :] = jnp.where(
                lane <= sub + TILE * t, top[t] * (scale * lax.rsqrt(pivots[t])), 0.0
            )
    a1, a2, a3 = three(f_ref[...])
    b1, b2, b3 = three(w_ref[...])
    along = (((1,), (1,)), ((), ()))
    wide = lax.dot_general(
        jnp.concatenate([a1, a2], axis=1),
        jnp.concatenate([jnp.concatenate([b1, b1], axis=1), jnp.concatenate([b2, b2], axis=1)], axis=0),
        along, preferred_element_type=F32,
    )
    small = lax.dot_general(
        jnp.concatenate([a1, a3], axis=1), jnp.concatenate([b3, b1], axis=1),
        along, preferred_element_type=F32,
    )
    out_ref[...] = wide[:, :VEC] + (wide[:, VEC:] + small)


def ortho_call(gram_matrix, filtered, scale):
    vmem = pl.BlockSpec(memory_space=pltpu.VMEM)
    return pl.pallas_call(
        functools.partial(ortho_kernel, scale),
        name="ortho",
        out_shape=jax.ShapeDtypeStruct((BLK, VEC), F32),
        in_specs=[vmem, vmem],
        out_specs=vmem,
        scratch_shapes=[pltpu.VMEM((VEC, VEC), F32)],
    )(gram_matrix, filtered)


def per_device(start_block, inverses, iface_rows, neighbors, couplings, pole_weights):
    filtered, gram_matrix = filter_call(
        neighbors.T, pole_weights, iface_rows, couplings,
        start_block.reshape(SUB, BLK, VEC), inverses[0],
    )
    return ortho_call(gram_matrix, filtered, math.sqrt(NSUB * SUB * BLK))


def solution(mesh):
    placed = (
        P("sub", None),
        P("pole", "sub", None, None),
        P("sub", None, None),
        P("sub", None),
        P("sub", None, None),
        P("pole"),
    )
    return jax.shard_map(
        per_device, mesh=mesh, in_specs=placed, out_specs=P(("sub", "pole"), None), check_vma=False
    )
```
